32 devices in a mesh: dp: 8 (over z, x), tensor: 4 (over y, core).
Axes of the slice: x: 2, y: 2, z: 4, core: 2. Of those that a mesh axis runs over, the one named last changes fastest.
Arguments:
- block_input: float32 [4096, 1024], P(('dp', 'tensor')), may hold values from -6 to 6
- seq_begin: int32 [4096], P('dp'), may hold values from 0 to 511, as said below
- group_fill: int32 [8], P('dp'), may hold values from 256 to 512, as said below
- attention_norm_gain: float32 [1024], P(('dp', 'tensor')), may hold values from 0.1 to 1.9
- attention_norm_bias: float32 [1024], P(('dp', 'tensor')), may hold values from -3 to 3
- qkv_weight: bfloat16 [1024, 3072], P('dp', 'tensor'), may hold values from -0.1875 to 0.1875
- qv_bias: bfloat16 [2048], P(('tensor', 'dp')), may hold values from -3 to 3
- dense_weight: bfloat16 [1024, 1024], P(('tensor', 'dp')), may hold values from -0.5 to 0.5
- dense_bias: float32 [1024], P(('dp', 'tensor')), may hold values from -3 to 3
- feedforward_norm_gain: float32 [1024], P(('dp', 'tensor')), may hold values from 0.1 to 1.9
- feedforward_norm_bias: float32 [1024], P(('dp', 'tensor')), may hold values from -3 to 3
- up_weight: bfloat16 [1024, 4096], P('dp', 'tensor'), may hold values from -0.1875 to 0.1875
- up_bias: bfloat16 [4096], P(('tensor', 'dp')), may hold values from -3 to 3
- down_weight: bfloat16 [4096, 1024], P(('tensor', 'dp')), may hold values from -0.09375 to 0.09375
- down_bias: float32 [1024], P(('dp', 'tensor')), may hold values from -3 to 3
- out_grad: float32 [4096, 1024], P(('dp', 'tensor')), may hold values from -6 to 6
Outputs:
- block_out: float32 [4096, 1024], P(('dp', 'tensor'))
- block_input_gradient: float32 [4096, 1024], P(('dp', 'tensor'))
- attention_gain_gradient: float32 [1024], P(('dp', 'tensor'))
- attn_bias_grad: float32 [1024], P(('dp', 'tensor'))
- qkv_weight_grad: float32 [1024, 3072], P('dp', 'tensor')
- qv_bias_grad: float32 [2048], P(('tensor', 'dp'))
- dense_weight_grad: float32 [1024, 1024], P(('tensor', 'dp'))
- dense_bias_grad: float32 [1024], P(('dp', 'tensor'))
- feedforward_gain_gradient: float32 [1024], P(('dp', 'tensor'))
- mlp_bias_grad: float32 [1024], P(('dp', 'tensor'))
- up_weight_grad: float32 [1024, 4096], P('dp', 'tensor')
- up_bias_grad: float32 [4096], P(('tensor', 'dp'))
- down_weight_grad: float32 [4096, 1024], P(('tensor', 'dp'))
- down_bias_grad: float32 [1024], P(('dp', 'tensor'))
The draws below stay inside these ranges and needn't reach their ends.
Inputs may be any that keep to these rules, and one draw needn't show every extreme that they name: For row i of a group, seq_begin is the row of the same group where the sequence of row i starts, at most i; rows at or beyond the group's fill have seq_begin equal to their own row. One group in each draw holds a single sequence of 512 rows. `group_fill`: one group in each draw is full.
All inputs are finite; a program needn't handle non-finite values.
Results may differ from the reference program's by a relative error of at most 0.018.
Values may be sent and summed in bfloat16 or wider, within the bound.
A program may use at most 128 MiB of HBM per device.

```python
import math
import jax
import jax.numpy as jnp
from jax import lax

D = 1024
HEADS = 16
FF = 4096
TOK_GRP = 512
TOKENS = 4096


def layout_tables(key):
    group_count = TOKENS // TOK_GRP
    fill_key = jax.random.fold_in(key, 11)
    full_key = jax.random.fold_in(key, 12)
    cut_key = jax.random.fold_in(key, 13)
    groups_idx = jnp.arange(group_count, dtype=jnp.int32)
    fills = jax.random.randint(fill_key, (group_count,), TOK_GRP // 2, TOK_GRP, dtype=jnp.int32)
    full_group = jax.random.randint(full_key, (), 0, group_count, dtype=jnp.int32)
    fills = jnp.where(groups_idx == full_group, TOK_GRP, fills).astype(jnp.int32)
    row_idx = jnp.arange(TOK_GRP, dtype=jnp.int32)[None, :]
    cuts = jax.random.randint(cut_key, (group_count, TOK_GRP), 0, TOK_GRP, dtype=jnp.int32) < 3
    cuts = cuts & (groups_idx[:, None] != full_group)
    marks = jnp.where(cuts | (row_idx == 0), row_idx, 0)
    begins = lax.cummax(marks, axis=1)
    begins = jnp.where(row_idx < fills[:, None], begins, row_idx)
    return (begins.reshape(-1).astype(jnp.int32), fills)


def draw_seq_begin(key, part):
    return layout_tables(key)[0]


def draw_group_fill(key, part):
    return layout_tables(key)[1]


def block_scale(own_key, extent, split, smallest, largest):
    loudness = 1.0
    for dim, shards_of in split:
        draws = jax.random.uniform(jax.random.fold_in(jax.random.fold_in(own_key, 6), dim), (shards_of,), jnp.float32, smallest / len(split), largest / len(split))
        loudness = loudness * jnp.repeat(jnp.exp(draws), extent[dim] // shards_of).reshape((-1,) + (1,) * (len(extent) - 1 - dim))
    return loudness


def scatter_about(own_key, shape, width, bound, shards=(), held_as=jnp.bfloat16):
    array = jax.random.normal(own_key, shape, jnp.float32) * width
    if len(shards) > 0:
        array = block_scale(own_key, shape, shards, -0.22, 0.18) * array
    return jnp.clip(array, min=-bound, max=bound).astype(held_as)


def setup_inputs(seed: int = 0) -> dict:
    splits = jax.random.split(jax.random.key(seed), 17)
    return {
        "block_input": scatter_about(splits[0], (TOKENS, D), 1.0, 6.0, ((0, 32),), jnp.float32),
        "seq_begin": draw_seq_begin(jax.random.fold_in(splits[16], 71), 0),
        "group_fill": draw_group_fill(jax.random.fold_in(splits[16], 71), 0),
        "attention_norm_gain": jnp.clip(1.0 + 0.18 * jax.random.normal(splits[3], (D,), jnp.float32), 0.1, 1.9),
        "attention_norm_bias": scatter_about(splits[4], (D,), 0.5, 3.0, ((0, 32),), jnp.float32),
        "qkv_weight": scatter_about(splits[5], (D, 3 * D), D ** -0.5, 0.1875, ((0, 8), (1, 4))),
        "qv_bias": scatter_about(splits[6], (2 * D,), 0.5, 3.0, ((0, 32),)),
        "dense_weight": scatter_about(splits[7], (D, D), (D // 8) ** -0.5, 0.5, ((0, 32),)),
        "dense_bias": scatter_about(splits[8], (D,), 0.5, 3.0, ((0, 32),), jnp.float32),
        "feedforward_norm_gain": jnp.clip(1.0 + 0.18 * jax.random.normal(splits[9], (D,), jnp.float32), 0.1, 1.9),
        "feedforward_norm_bias": scatter_about(splits[10], (D,), 0.5, 3.0, ((0, 32),), jnp.float32),
        "up_weight": scatter_about(splits[11], (D, FF), D ** -0.5, 0.1875, ((0, 8), (1, 4))),
        "up_bias": scatter_about(splits[12], (FF,), 0.5, 3.0, ((0, 32),)),
        "down_weight": scatter_about(splits[13], (FF, D), FF ** -0.5, 0.09375, ((0, 32),)),
        "down_bias": scatter_about(splits[14], (D,), 0.5, 3.0, ((0, 32),), jnp.float32),
        "out_grad": scatter_about(splits[15], (TOKENS, D), 1.0, 6.0, ((0, 32),), jnp.float32),
    }


EPSILON = 1e-05
MASKED_SCORE = -1e+30

def layer_normalize(hidden_row_count, norm_gain, norm_shift):
    row_mean = lax.optimization_barrier(jnp.mean(hidden_row_count, axis=-1, keepdims=True))
    centred = hidden_row_count - row_mean
    inv_std = lax.rsqrt(lax.optimization_barrier(jnp.mean(centred * centred, axis=-1, keepdims=True)) + EPSILON)
    normed = centred * inv_std
    return (normed * norm_gain + norm_shift, normed, inv_std)

def norm_backward_step(upstream, norm_gain, normed, inv_std):
    scaled = upstream * norm_gain
    return inv_std * (scaled - lax.optimization_barrier(jnp.mean(scaled, axis=-1, keepdims=True)) - normed * lax.optimization_barrier(jnp.mean(scaled * normed, axis=-1, keepdims=True)))

def gelu_tanh(values_in):
    return jax.nn.gelu(values_in, approximate=True)

def head_slopes(first_head, head_count):
    heads_idx = first_head + jnp.arange(head_count).astype(jnp.float32)
    return jnp.exp2(-8.0 * (heads_idx + 1.0) / HEADS)

def masked_scores(query_blk, key_all, slopes, row_start, begin_blk):
    row_count = query_blk.shape[0]
    key_count = key_all.shape[0]
    query_pos = row_start + jnp.arange(row_count, dtype=jnp.int32)
    key_pos = jnp.arange(key_count, dtype=jnp.int32)
    score_scale = 1.0 / math.sqrt(query_blk.shape[-1])
    logits = jnp.einsum('qhd,khd->hqk', query_blk.astype(jnp.float32), key_all.astype(jnp.float32)) * score_scale
    offset = (key_pos[None, :] - query_pos[:, None]).astype(jnp.float32)
    logits = logits + slopes[:, None, None] * offset[None, :, :]
    allowed = (key_pos[None, :] >= begin_blk[:, None]) & (key_pos[None, :] <= query_pos[:, None])
    return jnp.where(allowed[None, :, :], logits, MASKED_SCORE)

def attention_forward(queries, key_all, values, slopes, begins):
    total_rows = queries.shape[0]
    block_rows = min(512, total_rows)
    pieces = []
    totals = []
    for first_row in range(0, total_rows, block_rows):
        last_row = first_row + block_rows
        scores = masked_scores(queries[first_row:last_row], key_all, slopes, first_row, begins[first_row:last_row])
        row_top = lax.optimization_barrier(jnp.max(scores, axis=-1))
        log_total = row_top + jnp.log(lax.optimization_barrier(jnp.sum(jnp.exp(scores - row_top[..., None]), axis=-1)))
        attn_probs = jnp.exp(scores - log_total[..., None]).astype(jnp.bfloat16)
        pieces.append(jnp.einsum('hqk,khd->qhd', attn_probs.astype(jnp.float32), values.astype(jnp.float32)).astype(jnp.bfloat16))
        totals.append(log_total)
    return (jnp.concatenate(pieces, axis=0), jnp.concatenate(totals, axis=1))

def attention_backward(queries, key_all, values, slopes, begins, log_total, context, context_grad):
    total_rows = queries.shape[0]
    block_rows = min(512, total_rows)
    score_scale = 1.0 / math.sqrt(queries.shape[-1])
    key_grad = jnp.zeros(key_all.shape, jnp.float32)
    value_grad = jnp.zeros(values.shape, jnp.float32)
    query_parts = []
    for first_row in range(0, total_rows, block_rows):
        last_row = first_row + block_rows
        query_blk = queries[first_row:last_row]
        grad_blk = context_grad[first_row:last_row].astype(jnp.float32)
        scores = masked_scores(query_blk, key_all, slopes, first_row, begins[first_row:last_row])
        attn_probs = jnp.exp(scores - log_total[:, first_row:last_row, None])
        row_delta = lax.optimization_barrier(jnp.sum(grad_blk * context[first_row:last_row].astype(jnp.float32), axis=-1))
        probs_low = attn_probs.astype(jnp.bfloat16).astype(jnp.float32)
        value_grad = value_grad + jnp.einsum('hqk,qhd->khd', probs_low, grad_blk)
        prob_grad = jnp.einsum('qhd,khd->hqk', grad_blk, values.astype(jnp.float32))
        score_grad = (attn_probs * (prob_grad - jnp.transpose(row_delta)[:, :, None])).astype(jnp.bfloat16).astype(jnp.float32)
        query_parts.append(jnp.einsum('hqk,khd->qhd', score_grad, key_all.astype(jnp.float32)) * score_scale)
        key_grad = key_grad + jnp.einsum('hqk,qhd->khd', score_grad, query_blk.astype(jnp.float32)) * score_scale
    query_grad = jnp.concatenate(query_parts, axis=0)
    return jnp.stack([query_grad, key_grad, value_grad], axis=2).astype(jnp.bfloat16)

def group_pass(weights, slopes, hidden_row_count, grad_rows, begins, fill_value):
    attention_norm_gain, attention_norm_bias, qkv_weight, qv_bias, dense_weight, dense_bias, feedforward_norm_gain, feedforward_norm_bias, up_weight, up_bias, down_weight, down_bias = weights
    head_dim = D // HEADS
    group_rows = hidden_row_count.shape[0]
    normalized_input, first_standardized, first_inverse_deviation = layer_normalize(hidden_row_count, attention_norm_gain, attention_norm_bias)
    attn_in = normalized_input.astype(jnp.bfloat16)
    projected = jnp.dot(attn_in, qkv_weight, preferred_element_type=jnp.float32).reshape(group_rows, HEADS, 3, head_dim)
    bias_pair = qv_bias.astype(jnp.float32).reshape(HEADS, 2, head_dim)
    bias_full = jnp.stack([bias_pair[:, 0], jnp.zeros_like(bias_pair[:, 0]), bias_pair[:, 1]], axis=1)
    qkv_low = (projected + bias_full).astype(jnp.bfloat16)
    queries = qkv_low[:, :, 0]
    key_all = qkv_low[:, :, 1]
    values = qkv_low[:, :, 2]
    context, log_total = attention_forward(queries, key_all, values, slopes, begins)
    context_flat = context.reshape(group_rows, D)
    residual_middle = hidden_row_count + jnp.dot(context_flat, dense_weight, preferred_element_type=jnp.float32) + dense_bias
    normalized_middle, second_standardized, second_inverse_deviation = layer_normalize(residual_middle, feedforward_norm_gain, feedforward_norm_bias)
    mlp_in = normalized_middle.astype(jnp.bfloat16)
    pre_act = jnp.dot(mlp_in, up_weight, preferred_element_type=jnp.float32) + up_bias.astype(jnp.float32)
    act_value, act_back = jax.vjp(gelu_tanh, pre_act)
    activated = act_value.astype(jnp.bfloat16)
    block_out = residual_middle + jnp.dot(activated, down_weight, preferred_element_type=jnp.float32) + down_bias
    live_rows = (jnp.arange(group_rows) < fill_value).astype(jnp.float32)[:, None]
    running_gradient = grad_rows * live_rows
    down_bias_grad = lax.optimization_barrier(jnp.sum(running_gradient, axis=0))
    out_low = running_gradient.astype(jnp.bfloat16)
    down_weight_grad = jnp.dot(activated.T, out_low, preferred_element_type=jnp.float32)
    act_grad = jnp.dot(out_low, down_weight.T, preferred_element_type=jnp.float32)
    pre_grad = act_back(act_grad)[0].astype(jnp.bfloat16)
    up_weight_grad = jnp.dot(mlp_in.T, pre_grad, preferred_element_type=jnp.float32)
    up_bias_grad = lax.optimization_barrier(jnp.sum(pre_grad.astype(jnp.float32), axis=0))
    feedforward_input_gradient = jnp.dot(pre_grad, up_weight.T, preferred_element_type=jnp.float32)
    feedforward_gain_gradient = lax.optimization_barrier(jnp.sum(feedforward_input_gradient * second_standardized, axis=0))
    mlp_bias_grad = lax.optimization_barrier(jnp.sum(feedforward_input_gradient, axis=0))
    residual_middle_gradient = running_gradient + norm_backward_step(feedforward_input_gradient, feedforward_norm_gain, second_standardized, second_inverse_deviation)
    dense_bias_grad = lax.optimization_barrier(jnp.sum(residual_middle_gradient, axis=0))
    middle_low = residual_middle_gradient.astype(jnp.bfloat16)
    dense_weight_grad = jnp.dot(context_flat.T, middle_low, preferred_element_type=jnp.float32)
    context_grad = jnp.dot(middle_low, dense_weight.T, preferred_element_type=jnp.float32).astype(jnp.bfloat16).reshape(group_rows, HEADS, head_dim)
    qkv_grad = attention_backward(queries, key_all, values, slopes, begins, log_total, context, context_grad)
    qkv_grad_flat = qkv_grad.reshape(group_rows, 3 * D)
    qkv_weight_grad = jnp.dot(attn_in.T, qkv_grad_flat, preferred_element_type=jnp.float32)
    summed = lax.optimization_barrier(jnp.sum(qkv_grad.astype(jnp.float32), axis=0))
    qv_bias_grad = jnp.stack([summed[:, 0], summed[:, 2]], axis=1).reshape(2 * D)
    attention_input_gradient = jnp.dot(qkv_grad_flat, qkv_weight.T, preferred_element_type=jnp.float32)
    attention_gain_gradient = lax.optimization_barrier(jnp.sum(attention_input_gradient * first_standardized, axis=0))
    attn_bias_grad = lax.optimization_barrier(jnp.sum(attention_input_gradient, axis=0))
    block_input_gradient = residual_middle_gradient + norm_backward_step(attention_input_gradient, attention_norm_gain, first_standardized, first_inverse_deviation)
    grads = (attention_gain_gradient, attn_bias_grad, qkv_weight_grad, qv_bias_grad, dense_weight_grad, dense_bias_grad, feedforward_gain_gradient, mlp_bias_grad, up_weight_grad, up_bias_grad, down_weight_grad, down_bias_grad)
    return ((block_out, block_input_gradient), grads)

def reference(block_input, seq_begin, group_fill, attention_norm_gain, attention_norm_bias, qkv_weight, qv_bias, dense_weight, dense_bias, feedforward_norm_gain, feedforward_norm_bias, up_weight, up_bias, down_weight, down_bias, out_grad):
    group_count = TOKENS // TOK_GRP
    slopes = head_slopes(0.0, HEADS)
    weights = (attention_norm_gain, attention_norm_bias, qkv_weight, qv_bias, dense_weight, dense_bias, feedforward_norm_gain, feedforward_norm_bias, up_weight, up_bias, down_weight, down_bias)
    initial = tuple((jnp.zeros(weight_arr.shape, jnp.float32) for weight_arr in weights))

    def one_group(carry, inputs):
        hidden_row_count, grad_rows, begins, fill_value = inputs
        outputs, grads = group_pass(weights, slopes, hidden_row_count, grad_rows, begins, fill_value)
        return (tuple((total_val + new_val for total_val, new_val in zip(carry, grads))), outputs)
    inputs = (block_input.reshape(group_count, TOK_GRP, D), out_grad.reshape(group_count, TOK_GRP, D), seq_begin.reshape(group_count, TOK_GRP), group_fill)
    totals, outputs = lax.scan(one_group, initial, inputs)
    block_out = outputs[0].reshape(TOKENS, D)
    block_input_gradient = outputs[1].reshape(TOKENS, D)
    return (block_out, block_input_gradient, totals[0], totals[1], totals[2], totals[3], totals[4], totals[5], totals[6], totals[7], totals[8], totals[9], totals[10], totals[11])
```

```python
import functools
import math

import jax
import jax.numpy as jnp
from jax import lax
from jax.experimental import pallas as pl
from jax.experimental.pallas import tpu as pltpu
from jax.sharding import PartitionSpec as P

D = 1024
HEADS = 16


EPSILON = 1e-05
MASKED_SCORE = -1e30
CONTRACT_ROWS = (((0,), (0,)), ((), ()))
CONTRACT_COLS = (((1,), (1,)), ((), ()))


def layer_normalize(hidden_row_count, norm_gain, norm_shift):
    row_mean = jnp.mean(hidden_row_count, axis=-1, keepdims=True)
    centred = hidden_row_count - row_mean
    inv_std = lax.rsqrt(jnp.mean(centred * centred, axis=-1, keepdims=True) + EPSILON)
    normed = centred * inv_std
    return (normed * norm_gain + norm_shift, normed, inv_std)


def norm_backward_step(upstream, norm_gain, normed, inv_std):
    scaled = upstream * norm_gain
    return inv_std * (
        scaled
        - jnp.mean(scaled, axis=-1, keepdims=True)
        - normed * jnp.mean(scaled * normed, axis=-1, keepdims=True)
    )


def gelu_tanh(values_in):
    return jax.nn.gelu(values_in, approximate=True)


def head_slopes(first_head, head_count):
    heads_idx = first_head + jnp.arange(head_count).astype(jnp.float32)
    return jnp.exp2(-8.0 * (heads_idx + 1.0) / HEADS)


def masked_scores(query_blk, key_all, slopes, begin_blk):
    row_count = query_blk.shape[0]
    key_count = key_all.shape[0]
    query_pos = jnp.arange(row_count, dtype=jnp.int32)
    key_pos = jnp.arange(key_count, dtype=jnp.int32)
    score_scale = 1.0 / math.sqrt(query_blk.shape[-1])
    logits = (
        jnp.einsum("qhd,khd->hqk", query_blk, key_all, preferred_element_type=jnp.float32)
        * score_scale
    )
    offset = (key_pos[None, :] - query_pos[:, None]).astype(jnp.float32)
    logits = logits + slopes[:, None, None] * offset[None, :, :]
    allowed = (key_pos[None, :] >= begin_blk[:, None]) & (key_pos[None, :] <= query_pos[:, None])
    return jnp.where(allowed[None, :, :], logits, MASKED_SCORE)


def attention_forward(queries, key_all, values, slopes, begins):
    scores = masked_scores(queries, key_all, slopes, begins)
    row_top = jnp.max(scores, axis=-1)
    log_total = row_top + jnp.log(jnp.sum(jnp.exp(scores - row_top[..., None]), axis=-1))
    attn_probs = jnp.exp(scores - log_total[..., None]).astype(jnp.bfloat16)
    pieces = jnp.einsum(
        "hqk,khd->qhd", attn_probs, values, preferred_element_type=jnp.float32
    ).astype(jnp.bfloat16)
    return (pieces, log_total)


def attention_backward(queries, key_all, values, slopes, begins, log_total, context, context_grad):
    total_rows = queries.shape[0]
    block_rows = min(512, total_rows)
    score_scale = 1.0 / math.sqrt(queries.shape[-1])
    scores = masked_scores(queries, key_all, slopes, begins)
    attn_probs = jnp.exp(scores - log_total[:, 0:block_rows, None])
    row_delta = jnp.sum(context_grad.astype(jnp.float32) * context.astype(jnp.float32), axis=-1)
    value_grad = jnp.einsum(
        "hqk,qhd->khd",
        attn_probs.astype(jnp.bfloat16),
        context_grad,
        preferred_element_type=jnp.float32,
    )
    prob_grad = jnp.einsum("qhd,khd->hqk", context_grad, values, preferred_element_type=jnp.float32)
    score_grad = (attn_probs * (prob_grad - jnp.transpose(row_delta)[:, :, None])).astype(
        jnp.bfloat16
    )
    query_parts = (
        jnp.einsum("hqk,khd->qhd", score_grad, key_all, preferred_element_type=jnp.float32)
        * score_scale
    )
    key_grad = (
        jnp.einsum("hqk,qhd->khd", score_grad, queries, preferred_element_type=jnp.float32)
        * score_scale
    )
    return jnp.stack([query_parts, key_grad, value_grad], axis=2).astype(jnp.bfloat16)

MESH = pl.DeviceIdType.MESH
VECTOR_ROWS = 8
BF16 = jnp.bfloat16
F32 = jnp.float32


def place():
    return lax.axis_index("dp"), lax.axis_index("tensor")


def tensor_peers(t):
    h, c = t // 2, t % 2
    core = h * 2 + (1 - c)
    across = (1 - h) * 2 + c
    diagonal = (1 - h) * 2 + (1 - c)
    return core, across, diagonal


def enter(dp_count):
    d, t = place()
    barrier = pltpu.get_barrier_semaphore()
    for j in range(1, 4):
        pl.semaphore_signal(
            barrier, inc=1, device_id=(d, lax.rem(t + j, 4)), device_id_type=MESH
        )
    if dp_count == 1:
        pl.semaphore_wait(barrier, 3)
        return

    def greet(j, carry):
        pl.semaphore_signal(
            barrier, inc=1, device_id=(lax.rem(d + j, dp_count), t), device_id_type=MESH
        )
        return carry

    lax.fori_loop(1, dp_count, greet, 0)
    pl.semaphore_wait(barrier, 3 + dp_count - 1)


def remote(src, dst, send, recv, d, t):
    return pltpu.make_async_remote_copy(
        src_ref=src, dst_ref=dst, send_sem=send, recv_sem=recv, device_id=(d, t), device_id_type=MESH
    )


class VectorSum:
    def __init__(self, dp_count, dbuf, tbuf, dsend, drecv, tsend, trecv):
        self.dp_count = dp_count
        self.dbuf, self.tbuf = dbuf, tbuf
        self.dsend, self.drecv, self.tsend, self.trecv = dsend, drecv, tsend, trecv

    @staticmethod
    def scratch(dp_count, width):
        return [
            pltpu.VMEM((dp_count, VECTOR_ROWS, width), F32),
            pltpu.VMEM((4, VECTOR_ROWS, width), F32),
            pltpu.SemaphoreType.DMA((dp_count,)),
            pltpu.SemaphoreType.DMA((dp_count,)),
            pltpu.SemaphoreType.DMA((4,)),
            pltpu.SemaphoreType.DMA((4,)),
        ]

    def dcopy(self, j):
        d, t = place()
        return remote(
            self.dbuf.at[0], self.dbuf.at[j], self.dsend.at[j], self.drecv.at[j],
            lax.rem(d + j, self.dp_count), t,
        )

    def tcopy(self, j):
        d, t = place()
        return remote(
            self.tbuf.at[0], self.tbuf.at[j], self.tsend.at[j], self.trecv.at[j],
            d, lax.rem(t + j, 4),
        )

    def start(self, value):
        self.dbuf[0] = value

        def go(j, carry):
            self.dcopy(j).start()
            return carry

        lax.fori_loop(1, self.dp_count, go, 0)

    def middle(self):
        def wait(j, carry):
            self.dcopy(j).wait()
            return carry

        lax.fori_loop(1, self.dp_count, wait, 0)
        self.tbuf[0] = jnp.sum(self.dbuf[...], axis=0)
        for j in range(1, 4):
            self.tcopy(j).start()

    def finish(self):
        for j in range(1, 4):
            self.tcopy(j).wait()
        own = self.tbuf[0]
        total = own + self.tbuf[1] + self.tbuf[2] + self.tbuf[3]
        row = lax.broadcasted_iota(jnp.int32, own.shape, 0)
        return jnp.where(row < 6, total, own)


class TensorGather:
    def __init__(self, buf, send, recv):
        self.buf, self.send, self.recv = buf, send, recv
        d, t = place()
        core, across, diagonal = tensor_peers(t)
        half = buf.shape[1] // 2
        part = [pl.ds(k * half, half) for k in range(2)]
        at = lambda s, k: buf.at[s, part[k]]
        self.to_across = [
            remote(at(t, k), at(t, k), send.at[k], recv.at[k], d, across) for k in range(2)
        ]
        self.to_core = [
            remote(at(t, k), at(t, k), send.at[2 + k], recv.at[2 + k], d, core) for k in range(2)
        ]
        self.relay = [
            remote(at(across, k), at(across, k), send.at[4 + k], recv.at[4 + k], d, core)
            for k in range(2)
        ]

    @staticmethod
    def scratch():
        return [pltpu.SemaphoreType.DMA((6,)), pltpu.SemaphoreType.DMA((6,))]

    def start(self, value):
        _, t = place()
        self.buf[t] = value
        for c in self.to_across + self.to_core:
            c.start()

    def forward(self):
        for k in range(2):
            self.to_across[k].wait_recv()
            self.relay[k].start()

    def finish(self):
        for c in self.to_across:
            c.wait_send()
        for c in self.to_core + self.relay:
            c.wait()


class TensorScatter:
    def __init__(self, part, near, far, out, send, recv):
        self.part, self.near, self.far, self.out = part, near, far, out
        d, t = place()
        core, across, diagonal = tensor_peers(t)
        half = part.shape[1] // 2
        self.rows = [pl.ds(k * half, half) for k in range(2)]
        r = self.rows
        self.first = [
            remote(part.at[diagonal, r[k]], near.at[1, r[k]], send.at[k], recv.at[k], d, core)
            for k in range(2)
        ]
        self.own = [
            remote(part.at[core, r[k]], near.at[0, r[k]], send.at[2 + k], recv.at[2 + k], d, core)
            for k in range(2)
        ]
        self.second = [
            remote(out.at[r[k]], far.at[r[k]], send.at[4 + k], recv.at[4 + k], d, across)
            for k in range(2)
        ]

    @staticmethod
    def scratch(rows, width):
        return [
            pltpu.VMEM((2, rows, width), BF16),
            pltpu.VMEM((rows, width), BF16),
            pltpu.VMEM((rows, width), BF16),
            pltpu.SemaphoreType.DMA((6,)),
            pltpu.SemaphoreType.DMA((6,)),
        ]

    def start(self):
        for c in self.first + self.own:
            c.start()

    def middle(self):
        _, t = place()
        _, across, _ = tensor_peers(t)
        for k in range(2):
            self.first[k].wait_recv()
            r = self.rows[k]
            self.out[r] = (
                self.part[across, r].astype(F32) + self.near[1, r].astype(F32)
            ).astype(BF16)
            self.second[k].start()

    def finish(self):
        _, t = place()
        for c in self.first:
            c.wait_send()
        for c in self.own + self.second:
            c.wait()
        return (
            self.part[t].astype(F32) + self.near[0].astype(F32) + self.far[...].astype(F32)
        )


def gather_kernel(dp_count, *refs):
    (vec_ref, x_ref, og_ref, w0, w1, w2, w3,
     vec_out, attn_in, out_low, o0, o1, o2, o3,
     *scratch) = refs
    weights = list(zip((w0, w1, w2, w3), (o0, o1, o2, o3)))
    zsend, xsend, wrecv, lsem = scratch[:4]
    vsum = VectorSum(dp_count, *scratch[4:10])
    d, t = place()
    line, b = d // 2, d % 2
    line_count = dp_count // 2
    enter(dp_count)
    vsum.start(vec_ref[...])
    gather_x = TensorGather(attn_in, *scratch[10:12])
    gather_o = TensorGather(out_low, *scratch[12:14])

    def zcopy(w, way, step, blk, src):
        return remote(
            src, weights[w][1].at[blk * 2 + b], zsend.at[w, way, step],
            wrecv.at[w, blk * 2 + b], (line + (1 if way == 0 else -1)) * 2 + b, t,
        )

    def xcopy(w, blk, src):
        return remote(
            src, weights[w][1].at[blk * 2 + b], xsend.at[w, blk], wrecv.at[w, blk * 2 + b],
            line * 2 + (1 - b), t,
        )

    def local(w):
        return pltpu.make_async_copy(weights[w][0], weights[w][1].at[d], lsem.at[w])

    for w in range(4):
        own = weights[w][0]

        @pl.when(line + 1 < line_count)
        def _():
            zcopy(w, 0, 0, line, own).start()

        @pl.when(line > 0)
        def _():
            zcopy(w, 1, 0, line, own).start()

        xcopy(w, line, own).start()
        local(w).start()
    gather_o.start(og_ref[...])
    vsum.middle()
    vec = vsum.finish()
    vec_out[...] = vec
    normed = layer_normalize(x_ref[...], vec[0:1], vec[1:2])[0]
    gather_x.start(normed.astype(BF16))

    def relay(step, carry):
        for w in range(4):
            for way in range(2):
                blk = line - step if way == 0 else line + step
                valid = (blk >= 0) if way == 0 else (blk < line_count)
                more = (line + 1 < line_count) if way == 0 else (line > 0)

                @pl.when(valid)
                def _():
                    src = weights[w][1].at[blk * 2 + b]
                    zcopy(w, way, step, blk, src).wait_recv()

                    @pl.when(more)
                    def _():
                        zcopy(w, way, step, blk, src).start()

                    xcopy(w, blk, src).start()
        return carry

    lax.fori_loop(1, line_count, relay, 0)
    gather_o.forward()
    gather_x.forward()
    for w in range(4):
        local(w).wait()

        @pl.when(line + 1 < line_count)
        def _():
            zcopy(w, 0, 0, line, weights[w][0]).wait_send()

        @pl.when(line > 0)
        def _():
            zcopy(w, 1, 0, line, weights[w][0]).wait_send()

    def drain(step, carry):
        for w in range(4):
            for way in range(2):
                blk = line - step if way == 0 else line + step
                valid = (blk >= 0) if way == 0 else (blk < line_count)
                more = (line + 1 < line_count) if way == 0 else (line > 0)

                @pl.when(valid & more)
                def _():
                    zcopy(w, way, step, blk, weights[w][1].at[blk * 2 + b]).wait_send()
        return carry

    lax.fori_loop(1, line_count, drain, 0)

    def drain_x(blk, carry):
        for w in range(4):
            xcopy(w, blk, weights[w][0]).wait_send()
            remote(
                weights[w][0], weights[w][1].at[blk * 2 + (1 - b)], xsend.at[w, blk],
                wrecv.at[w, blk * 2 + (1 - b)], line * 2 + (1 - b), t,
            ).wait_recv()
        return carry

    lax.fori_loop(0, line_count, drain_x, 0)
    gather_o.finish()
    gather_x.finish()


def params(collective_id):
    return pltpu.CompilerParams(
        collective_id=collective_id, has_side_effects=True, vmem_limit_bytes=60 * 1024 * 1024
    )


def vmem(count):
    return [pl.BlockSpec(memory_space=pltpu.VMEM)] * count


def gather_all(dp_count, vec, x, og, weights):
    rows, width = x.shape
    line_count = dp_count // 2
    shape = jax.ShapeDtypeStruct
    return pl.pallas_call(
        functools.partial(gather_kernel, dp_count),
        out_shape=[
            shape(vec.shape, F32),
            shape((4, rows, width), BF16),
            shape((4, rows, width), BF16),
        ] + [shape((dp_count,) + w.shape, BF16) for w in weights],
        in_specs=vmem(7),
        out_specs=vmem(3) + [pl.BlockSpec(memory_space=pl.ANY)] * 4,
        scratch_shapes=[
            pltpu.SemaphoreType.DMA((4, 2, line_count)),
            pltpu.SemaphoreType.DMA((4, line_count)),
            pltpu.SemaphoreType.DMA((4, dp_count)),
            pltpu.SemaphoreType.DMA((4,)),
        ] + VectorSum.scratch(dp_count, width) + TensorGather.scratch() + TensorGather.scratch(),
        compiler_params=params(1),
        name="gather_all",
    )(vec, x, og, *weights)


def middle_kernel(part, x_ref, vec_ref, middle_ref, mlp_in, *scratch):
    enter(1)
    scatter = TensorScatter(part, *scratch[:5])
    gather = TensorGather(mlp_in, *scratch[5:7])
    scatter.start()
    scatter.middle()
    base = x_ref[...] + vec_ref[2:3]
    middle = base + scatter.finish()
    middle_ref[...] = middle
    gather.start(layer_normalize(middle, vec_ref[3:4], vec_ref[4:5])[0].astype(BF16))
    gather.forward()
    gather.finish()


def middle_exchange(part, x, vec):
    rows, width = x.shape
    shape = jax.ShapeDtypeStruct
    return pl.pallas_call(
        middle_kernel,
        out_shape=[shape(x.shape, F32), shape((4, rows, width), BF16)],
        in_specs=vmem(3),
        out_specs=vmem(2),
        scratch_shapes=TensorScatter.scratch(rows, width) + TensorGather.scratch(),
        compiler_params=params(2),
        name="middle_exchange",
    )(part, x, vec)


def put_rows(base, values):
    row = lax.broadcasted_iota(jnp.int32, base.shape, 0)
    for index, value in values:
        base = jnp.where(row == index, value, base)
    return base


def column_sum(value):
    return jnp.sum(value, axis=0, keepdims=True)


def back_kernel(part, middle_ref, run_ref, vec_ref, grad_ref, low, sums_ref, *scratch):
    enter(1)
    scatter = TensorScatter(part, *scratch[:5])
    gather = TensorGather(low, *scratch[5:7])
    scatter.start()
    scatter.middle()
    _, normed, inverse = layer_normalize(middle_ref[...], vec_ref[3:4], vec_ref[4:5])
    upstream = scatter.finish()
    grad = run_ref[...] + norm_backward_step(upstream, vec_ref[3:4], normed, inverse)
    grad_ref[...] = grad
    gather.start(grad.astype(BF16))
    sums_ref[...] = put_rows(
        jnp.zeros(sums_ref.shape, F32),
        [
            (2, column_sum(grad)),
            (3, column_sum(upstream * normed)),
            (4, column_sum(upstream)),
            (5, column_sum(run_ref[...])),
        ],
    )
    gather.forward()
    gather.finish()


def back_exchange(part, middle, run, vec):
    rows, width = middle.shape
    shape = jax.ShapeDtypeStruct
    return pl.pallas_call(
        back_kernel,
        out_shape=[
            shape(middle.shape, F32),
            shape((4, rows, width), BF16),
            shape((VECTOR_ROWS, width), F32),
        ],
        in_specs=vmem(4),
        out_specs=vmem(3),
        scratch_shapes=TensorScatter.scratch(rows, width) + TensorGather.scratch(),
        compiler_params=params(3),
        name="back_exchange",
    )(part, middle, run, vec)


def reduce_kernel(dp_count, *refs):
    (part_in, part_out, x_ref, middle_ref, mgrad_ref, vec_ref, sums_ref,
     g0, g1, g2, g3,
     block_out, input_grad, sums_out, o0, o1, o2, o3,
     *scratch) = refs
    grads, outs = (g0, g1, g2, g3), (o0, o1, o2, o3)
    held, below, above = scratch[0:4], scratch[4:8], scratch[8:12]
    xsend, xrecv, zsend, zrecv = scratch[12:16]
    vsum = VectorSum(dp_count, *scratch[16:22])
    d, t = place()
    line, b = d // 2, d % 2
    line_count = dp_count // 2
    enter(dp_count)
    scatter_in = TensorScatter(part_in, *scratch[22:27])
    scatter_out = TensorScatter(part_out, *scratch[27:32])

    def xcopy(w, target):
        return remote(
            grads[w].at[target * 2 + (1 - b)], held[w].at[target], xsend.at[w, target],
            xrecv.at[w, target], line * 2 + (1 - b), t,
        )

    def zcopy(w, way, target):
        dst = (below if way == 0 else above)[w]
        return remote(
            held[w].at[target], dst.at[target], zsend.at[w, target],
            zrecv.at[w, way, target], (line + (1 if way == 0 else -1)) * 2 + b, t,
        )

    def each_target(act):
        def step(i, carry):
            @pl.when(line_count - 1 - i > line)
            def _():
                act(0, line_count - 1 - i)

            @pl.when(i < line)
            def _():
                act(1, i)

            return carry

        lax.fori_loop(0, line_count - 1, step, 0)

    def send_x(way, target):
        for w in range(4):
            xcopy(w, target).start()

    scatter_in.start()
    each_target(send_x)
    send_x(0, line)
    scatter_in.middle()
    scatter_out.start()
    scatter_out.middle()
    _, normed, inverse = layer_normalize(x_ref[...], vec_ref[0:1], vec_ref[1:2])
    upstream = scatter_in.finish()
    input_grad[...] = mgrad_ref[...] + norm_backward_step(
        upstream, vec_ref[0:1], normed, inverse
    )
    vsum.start(
        put_rows(
            sums_ref[...], [(0, column_sum(upstream * normed)), (1, column_sum(upstream))]
        )
    )

    def reduce(way, target):
        for w in range(4):
            xcopy(w, target).wait_recv()
            dst = (below if way == 0 else above)[w]
            has = (line > 0) if way == 0 else (line + 1 < line_count)

            @pl.when(has)
            def _():
                zcopy(w, way, target).wait_recv()
                held[w][target] = (
                    grads[w][target * 2 + b].astype(F32)
                    + held[w][target].astype(F32)
                    + dst[target].astype(F32)
                ).astype(BF16)

            @pl.when(jnp.logical_not(has))
            def _():
                held[w][target] = (
                    grads[w][target * 2 + b].astype(F32) + held[w][target].astype(F32)
                ).astype(BF16)

            zcopy(w, way, target).start()

    each_target(reduce)
    block_out[...] = middle_ref[...] + scatter_out.finish() + vec_ref[5:6]
    vsum.middle()
    for w in range(4):
        xcopy(w, line).wait_recv()
        outs[w][...] = grads[w][d].astype(F32) + held[w][line].astype(F32)

        @pl.when(line > 0)
        def _():
            zcopy(w, 0, line).wait_recv()
            outs[w][...] += below[w][line].astype(F32)

        @pl.when(line + 1 < line_count)
        def _():
            zcopy(w, 1, line).wait_recv()
            outs[w][...] += above[w][line].astype(F32)

    sums_out[...] = vsum.finish()

    def drain(way, target):
        for w in range(4):
            zcopy(w, way, target).wait_send()
            xcopy(w, target).wait_send()

    each_target(drain)
    for w in range(4):
        xcopy(w, line).wait_send()


def reduce_all(dp_count, part_in, part_out, x, middle, mgrad, vec, sums, grads):
    rows, width = x.shape
    line_count = dp_count // 2
    shape = jax.ShapeDtypeStruct
    blocks = [g.shape[1:] for g in grads]
    lines = [pltpu.VMEM((line_count,) + s, BF16) for s in blocks]
    return pl.pallas_call(
        functools.partial(reduce_kernel, dp_count),
        out_shape=[shape(x.shape, F32), shape(x.shape, F32), shape(vec.shape, F32)]
        + [shape(s, F32) for s in blocks],
        in_specs=vmem(11),
        out_specs=vmem(7),
        scratch_shapes=lines * 3
        + [
            pltpu.SemaphoreType.DMA((4, line_count)),
            pltpu.SemaphoreType.DMA((4, line_count)),
            pltpu.SemaphoreType.DMA((4, line_count)),
            pltpu.SemaphoreType.DMA((4, 2, line_count)),
        ]
        + VectorSum.scratch(dp_count, width)
        + TensorScatter.scratch(rows, width)
        + TensorScatter.scratch(rows, width),
        compiler_params=params(4),
        name="reduce_all",
    )(part_in, part_out, x, middle, mgrad, vec, sums, *grads)


def per_device(
    dp_count,
    block_input,
    seq_begin,
    group_fill,
    attention_norm_gain,
    attention_norm_bias,
    qkv_weight,
    qv_bias,
    dense_weight,
    dense_bias,
    feedforward_norm_gain,
    feedforward_norm_bias,
    up_weight,
    up_bias,
    down_weight,
    down_bias,
    out_grad,
):
    head_dim = D // HEADS
    own_rows, width = block_input.shape
    group_rows = seq_begin.shape[0]
    dp_index, tensor_index = lax.axis_index("dp"), lax.axis_index("tensor")
    shard = dp_index * 4 + tensor_index
    norm_vectors = jnp.stack(
        [
            attention_norm_gain,
            attention_norm_bias,
            dense_bias,
            feedforward_norm_gain,
            feedforward_norm_bias,
            down_bias,
        ]
    )
    piece = norm_vectors.shape[1]
    up_piece, qv_piece = up_bias.shape[0], qv_bias.shape[0]
    vec = jnp.zeros((VECTOR_ROWS, width), F32)
    vec = lax.dynamic_update_slice(vec, norm_vectors, (0, shard * piece))
    vec = lax.dynamic_update_slice(vec, up_bias.astype(F32)[None], (6, dp_index * up_piece))
    vec = lax.dynamic_update_slice(vec, qv_bias.astype(F32)[None], (7, dp_index * qv_piece))
    row_ids = tensor_index * own_rows + jnp.arange(own_rows, dtype=jnp.int32)
    live_rows = (row_ids < group_fill[0]).astype(jnp.float32)[:, None]
    running_gradient = out_grad * live_rows
    vec, attn_in, out_low, qkv_full, dense_full, up_full, down_full = gather_all(
        dp_count,
        vec,
        block_input,
        running_gradient.astype(BF16),
        (qkv_weight, dense_weight, up_weight, down_weight),
    )
    attn_in = attn_in.reshape(group_rows, width)
    out_low = out_low.reshape(group_rows, width)
    qkv_full, dense_full, up_full, down_full = (
        w.reshape(-1, w.shape[-1]) for w in (qkv_full, dense_full, up_full, down_full)
    )
    local_heads = qkv_full.shape[1] // (3 * head_dim)
    slopes = head_slopes((tensor_index * local_heads).astype(jnp.float32), local_heads)
    projected = jnp.dot(attn_in, qkv_full, preferred_element_type=jnp.float32).reshape(
        group_rows, local_heads, 3, head_dim
    )
    bias_pair = vec[7, : 2 * local_heads * head_dim].reshape(local_heads, 2, head_dim)
    bias_full = jnp.stack(
        [bias_pair[:, 0], jnp.zeros_like(bias_pair[:, 0]), bias_pair[:, 1]], axis=1
    )
    qkv_low = (projected + bias_full).astype(jnp.bfloat16)
    queries = qkv_low[:, :, 0]
    key_all = qkv_low[:, :, 1]
    values = qkv_low[:, :, 2]
    context, log_total = attention_forward(queries, key_all, values, slopes, seq_begin)
    context_flat = context.reshape(group_rows, local_heads * head_dim)
    attn_part = jnp.dot(context_flat, dense_full, preferred_element_type=jnp.float32).astype(BF16)
    residual_middle, mlp_in = middle_exchange(
        attn_part.reshape(4, own_rows, width), block_input, vec
    )
    mlp_in = mlp_in.reshape(group_rows, width)
    pre_act = jnp.dot(mlp_in, up_full, preferred_element_type=jnp.float32) + vec[6]
    act_value, act_back = jax.vjp(gelu_tanh, pre_act)
    activated = act_value.astype(jnp.bfloat16)
    act_grad = lax.dot_general(
        out_low, down_full, CONTRACT_COLS, preferred_element_type=jnp.float32
    )
    pre_grad = act_back(act_grad)[0].astype(jnp.bfloat16)
    mlp_in_part = lax.dot_general(
        pre_grad, up_full, CONTRACT_COLS, preferred_element_type=jnp.float32
    ).astype(BF16)
    residual_middle_gradient, middle_low, sums = back_exchange(
        mlp_in_part.reshape(4, own_rows, width), residual_middle, running_gradient, vec
    )
    middle_low = middle_low.reshape(group_rows, width)
    mlp_part = jnp.dot(activated, down_full, preferred_element_type=jnp.float32).astype(BF16)
    down_grad = lax.dot_general(
        activated, out_low, CONTRACT_ROWS, preferred_element_type=jnp.float32
    )
    up_grad = lax.dot_general(mlp_in, pre_grad, CONTRACT_ROWS, preferred_element_type=jnp.float32)
    up_shift_grad = jnp.sum(pre_grad.astype(jnp.float32), axis=0)
    dense_grad = lax.dot_general(
        context_flat, middle_low, CONTRACT_ROWS, preferred_element_type=jnp.float32
    )
    context_grad = lax.dot_general(
        middle_low, dense_full, CONTRACT_COLS, preferred_element_type=jnp.float32
    )
    context_grad = context_grad.astype(jnp.bfloat16).reshape(group_rows, local_heads, head_dim)
    qkv_grad = attention_backward(
        queries, key_all, values, slopes, seq_begin, log_total, context, context_grad
    )
    qkv_grad_flat = qkv_grad.reshape(group_rows, 3 * local_heads * head_dim)
    qkv_grad_sum = lax.dot_general(
        attn_in, qkv_grad_flat, CONTRACT_ROWS, preferred_element_type=jnp.float32
    )
    summed = jnp.sum(qkv_grad.astype(jnp.float32), axis=0)
    qv_grad = jnp.stack([summed[:, 0], summed[:, 2]], axis=1).reshape(2 * local_heads * head_dim)
    attn_in_part = lax.dot_general(
        qkv_grad_flat, qkv_full, CONTRACT_COLS, preferred_element_type=jnp.float32
    ).astype(BF16)
    sums = lax.dynamic_update_slice(sums, up_shift_grad[None], (6, 0))
    sums = lax.dynamic_update_slice(sums, qv_grad[None], (7, 0))
    grads = tuple(
        g.astype(BF16).reshape(dp_count, -1, g.shape[-1])
        for g in (qkv_grad_sum, dense_grad, up_grad, down_grad)
    )
    block_out, block_input_gradient, sums, qkv_out, dense_out, up_out, down_out = reduce_all(
        dp_count,
        attn_in_part.reshape(4, own_rows, width),
        mlp_part.reshape(4, own_rows, width),
        block_input,
        residual_middle,
        residual_middle_gradient,
        vec,
        sums,
        grads,
    )
    vectors = lax.dynamic_slice(sums, (0, shard * piece), (6, piece))
    up_shift_out = lax.dynamic_slice(sums, (6, dp_index * up_piece), (1, up_piece))[0]
    qv_out = lax.dynamic_slice(sums, (7, dp_index * qv_piece), (1, qv_piece))[0]
    return (
        block_out,
        block_input_gradient,
        vectors[0],
        vectors[1],
        qkv_out,
        qv_out,
        dense_out,
        vectors[2],
        vectors[3],
        vectors[4],
        up_out,
        up_shift_out,
        down_out,
        vectors[5],
    )


def solution(mesh):
    return jax.shard_map(
        functools.partial(per_device, mesh.shape["dp"]),
        mesh=mesh,
        in_specs=(
            P(("dp", "tensor"), None),
            P("dp"),
            P("dp"),
            P(("dp", "tensor")),
            P(("dp", "tensor")),
            P("dp", "tensor"),
            P(("tensor", "dp")),
            P(("tensor", "dp"), None),
            P(("dp", "tensor")),
            P(("dp", "tensor")),
            P(("dp", "tensor")),
            P("dp", "tensor"),
            P(("tensor", "dp")),
            P(("tensor", "dp"), None),
            P(("dp", "tensor")),
            P(("dp", "tensor"), None),
        ),
        out_specs=(
            P(("dp", "tensor"), None),
            P(("dp", "tensor"), None),
            P(("dp", "tensor")),
            P(("dp", "tensor")),
            P("dp", "tensor"),
            P(("tensor", "dp")),
            P(("tensor", "dp"), None),
            P(("dp", "tensor")),
            P(("dp", "tensor")),
            P(("dp", "tensor")),
            P("dp", "tensor"),
            P(("tensor", "dp")),
            P(("tensor", "dp"), None),
            P(("dp", "tensor")),
        ),
        check_vma=False,
    )
```

```python
import functools
import math

import jax
import jax.numpy as jnp
from jax import lax
from jax.experimental import pallas as pl
from jax.experimental.pallas import tpu as pltpu
from jax.sharding import PartitionSpec as P

D = 1024
HEADS = 16


EPSILON = 1e-05
MASKED_SCORE = -1e30
CONTRACT_ROWS = (((0,), (0,)), ((), ()))
CONTRACT_COLS = (((1,), (1,)), ((), ()))


def layer_normalize(hidden_row_count, norm_gain, norm_shift):
    row_mean = jnp.mean(hidden_row_count, axis=-1, keepdims=True)
    centred = hidden_row_count - row_mean
    inv_std = lax.rsqrt(jnp.mean(centred * centred, axis=-1, keepdims=True) + EPSILON)
    normed = centred * inv_std
    return (normed * norm_gain + norm_shift, normed, inv_std)


def norm_backward_step(upstream, norm_gain, normed, inv_std):
    scaled = upstream * norm_gain
    return inv_std * (
        scaled
        - jnp.mean(scaled, axis=-1, keepdims=True)
        - normed * jnp.mean(scaled * normed, axis=-1, keepdims=True)
    )


def gelu_tanh(values_in):
    return jax.nn.gelu(values_in, approximate=True)


def head_slopes(first_head, head_count):
    heads_idx = first_head + jnp.arange(head_count).astype(jnp.float32)
    return jnp.exp2(-8.0 * (heads_idx + 1.0) / HEADS)


def masked_scores(query_blk, key_all, slopes, begin_blk):
    row_count = query_blk.shape[0]
    key_count = key_all.shape[0]
    query_pos = jnp.arange(row_count, dtype=jnp.int32)
    key_pos = jnp.arange(key_count, dtype=jnp.int32)
    score_scale = 1.0 / math.sqrt(query_blk.shape[-1])
    logits = (
        jnp.einsum("qhd,khd->hqk", query_blk, key_all, preferred_element_type=jnp.float32)
        * score_scale
    )
    offset = (key_pos[None, :] - query_pos[:, None]).astype(jnp.float32)
    logits = logits + slopes[:, None, None] * offset[None, :, :]
    allowed = (key_pos[None, :] >= begin_blk[:, None]) & (key_pos[None, :] <= query_pos[:, None])
    return jnp.where(allowed[None, :, :], logits, MASKED_SCORE)


def attention_forward(queries, key_all, values, slopes, begins):
    scores = masked_scores(queries, key_all, slopes, begins)
    row_top = jnp.max(scores, axis=-1)
    log_total = row_top + jnp.log(jnp.sum(jnp.exp(scores - row_top[..., None]), axis=-1))
    attn_probs = jnp.exp(scores - log_total[..., None]).astype(jnp.bfloat16)
    pieces = jnp.einsum(
        "hqk,khd->qhd", attn_probs, values, preferred_element_type=jnp.float32
    ).astype(jnp.bfloat16)
    return (pieces, log_total)


def attention_backward(queries, key_all, values, slopes, begins, log_total, context, context_grad):
    total_rows = queries.shape[0]
    block_rows = min(512, total_rows)
    score_scale = 1.0 / math.sqrt(queries.shape[-1])
    scores = masked_scores(queries, key_all, slopes, begins)
    attn_probs = jnp.exp(scores - log_total[:, 0:block_rows, None])
    row_delta = jnp.sum(context_grad.astype(jnp.float32) * context.astype(jnp.float32), axis=-1)
    value_grad = jnp.einsum(
        "hqk,qhd->khd",
        attn_probs.astype(jnp.bfloat16),
        context_grad,
        preferred_element_type=jnp.float32,
    )
    prob_grad = jnp.einsum("qhd,khd->hqk", context_grad, values, preferred_element_type=jnp.float32)
    score_grad = (attn_probs * (prob_grad - jnp.transpose(row_delta)[:, :, None])).astype(
        jnp.bfloat16
    )
    query_parts = (
        jnp.einsum("hqk,khd->qhd", score_grad, key_all, preferred_element_type=jnp.float32)
        * score_scale
    )
    key_grad = (
        jnp.einsum("hqk,qhd->khd", score_grad, queries, preferred_element_type=jnp.float32)
        * score_scale
    )
    return jnp.stack([query_parts, key_grad, value_grad], axis=2).astype(jnp.bfloat16)

MESH = pl.DeviceIdType.MESH
VECTOR_ROWS = 8
BF16 = jnp.bfloat16
F32 = jnp.float32


def place():
    return lax.axis_index("dp"), lax.axis_index("tensor")


def tensor_peers(t):
    h, c = t // 2, t % 2
    core = h * 2 + (1 - c)
    across = (1 - h) * 2 + c
    diagonal = (1 - h) * 2 + (1 - c)
    return core, across, diagonal


def enter(dp_count):
    d, t = place()
    barrier = pltpu.get_barrier_semaphore()
    for j in range(1, 4):
        pl.semaphore_signal(
            barrier, inc=1, device_id=(d, lax.rem(t + j, 4)), device_id_type=MESH
        )
    if dp_count == 1:
        pl.semaphore_wait(barrier, 3)
        return

    def greet(j, carry):
        pl.semaphore_signal(
            barrier, inc=1, device_id=(lax.rem(d + j, dp_count), t), device_id_type=MESH
        )
        return carry

    lax.fori_loop(1, dp_count, greet, 0)
    pl.semaphore_wait(barrier, 3 + dp_count - 1)


def remote(src, dst, send, recv, d, t):
    return pltpu.make_async_remote_copy(
        src_ref=src, dst_ref=dst, send_sem=send, recv_sem=recv, device_id=(d, t), device_id_type=MESH
    )


class VectorSum:
    def __init__(self, dp_count, dbuf, tbuf, dsend, drecv, tsend, trecv):
        self.dp_count = dp_count
        self.dbuf, self.tbuf = dbuf, tbuf
        self.dsend, self.drecv, self.tsend, self.trecv = dsend, drecv, tsend, trecv

    @staticmethod
    def scratch(dp_count, width):
        return [
            pltpu.VMEM((dp_count, VECTOR_ROWS, width), F32),
            pltpu.VMEM((4, VECTOR_ROWS, width), F32),
            pltpu.SemaphoreType.DMA((dp_count,)),
            pltpu.SemaphoreType.DMA((dp_count,)),
            pltpu.SemaphoreType.DMA((4,)),
            pltpu.SemaphoreType.DMA((4,)),
        ]

    def dcopy(self, j):
        d, t = place()
        return remote(
            self.dbuf.at[0], self.dbuf.at[j], self.dsend.at[j], self.drecv.at[j],
            lax.rem(d + j, self.dp_count), t,
        )

    def tcopy(self, j):
        d, t = place()
        return remote(
            self.tbuf.at[0], self.tbuf.at[j], self.tsend.at[j], self.trecv.at[j],
            d, lax.rem(t + j, 4),
        )

    def start(self, value):
        self.dbuf[0] = value

        def go(j, carry):
            self.dcopy(j).start()
            return carry

        lax.fori_loop(1, self.dp_count, go, 0)

    def middle(self):
        def wait(j, carry):
            self.dcopy(j).wait()
            return carry

        lax.fori_loop(1, self.dp_count, wait, 0)
        self.tbuf[0] = jnp.sum(self.dbuf[...], axis=0)
        for j in range(1, 4):
            self.tcopy(j).start()

    def finish(self):
        for j in range(1, 4):
            self.tcopy(j).wait()
        own = self.tbuf[0]
        total = own + self.tbuf[1] + self.tbuf[2] + self.tbuf[3]
        row = lax.broadcasted_iota(jnp.int32, own.shape, 0)
        return jnp.where(row < 6, total, own)


class TensorGather:
    def __init__(self, buf, send, recv):
        self.buf, self.send, self.recv = buf, send, recv
        d, t = place()
        core, across, diagonal = tensor_peers(t)
        half = buf.shape[1] // 2
        part = [pl.ds(k * half, half) for k in range(2)]
        at = lambda s, k: buf.at[s, part[k]]
        self.to_across = [
            remote(at(t, k), at(t, k), send.at[k], recv.at[k], d, across) for k in range(2)
        ]
        self.to_core = [
            remote(at(t, k), at(t, k), send.at[2 + k], recv.at[2 + k], d, core) for k in range(2)
        ]
        self.relay = [
            remote(at(across, k), at(across, k), send.at[4 + k], recv.at[4 + k], d, core)
            for k in range(2)
        ]

    @staticmethod
    def scratch():
        return [pltpu.SemaphoreType.DMA((6,)), pltpu.SemaphoreType.DMA((6,))]

    def start(self, value):
        _, t = place()
        self.buf[t] = value
        for c in self.to_across + self.to_core:
            c.start()

    def forward(self):
        for k in range(2):
            self.to_across[k].wait_recv()
            self.relay[k].start()

    def finish(self):
        for c in self.to_across:
            c.wait_send()
        for c in self.to_core + self.relay:
            c.wait()


class TensorScatter:
    def __init__(self, part, near, far, out, send, recv):
        self.part, self.near, self.far, self.out = part, near, far, out
        d, t = place()
        core, across, diagonal = tensor_peers(t)
        half = part.shape[1] // 2
        self.rows = [pl.ds(k * half, half) for k in range(2)]
        r = self.rows
        self.first = [
            remote(part.at[diagonal, r[k]], near.at[1, r[k]], send.at[k], recv.at[k], d, core)
            for k in range(2)
        ]
        self.own = [
            remote(part.at[core, r[k]], near.at[0, r[k]], send.at[2 + k], recv.at[2 + k], d, core)
            for k in range(2)
        ]
        self.second = [
            remote(out.at[r[k]], far.at[r[k]], send.at[4 + k], recv.at[4 + k], d, across)
            for k in range(2)
        ]

    @staticmethod
    def scratch(rows, width):
        return [
            pltpu.VMEM((2, rows, width), BF16),
            pltpu.VMEM((rows, width), BF16),
            pltpu.VMEM((rows, width), BF16),
            pltpu.SemaphoreType.DMA((6,)),
            pltpu.SemaphoreType.DMA((6,)),
        ]

    def start(self):
        for c in self.first + self.own:
            c.start()

    def middle(self):
        _, t = place()
        _, across, _ = tensor_peers(t)
        for k in range(2):
            self.first[k].wait_recv()
            r = self.rows[k]
            self.out[r] = (
                self.part[across, r].astype(F32) + self.near[1, r].astype(F32)
            ).astype(BF16)
            self.second[k].start()

    def finish(self):
        _, t = place()
        for c in self.first:
            c.wait_send()
        for c in self.own + self.second:
            c.wait()
        return (
            self.part[t].astype(F32) + self.near[0].astype(F32) + self.far[...].astype(F32)
        )


class LineGather:
    def __init__(self, dp_count, weights, zsend, xsend, wrecv, lsem):
        self.weights, self.line_count = weights, dp_count // 2
        self.zsend, self.xsend, self.wrecv, self.lsem = zsend, xsend, wrecv, lsem
        self.d, self.t = place()
        self.line, self.b = self.d // 2, self.d % 2

    @staticmethod
    def scratch(dp_count, count):
        return [
            pltpu.SemaphoreType.DMA((count, 2, dp_count // 2)),
            pltpu.SemaphoreType.DMA((count, dp_count // 2)),
            pltpu.SemaphoreType.DMA((count, dp_count)),
            pltpu.SemaphoreType.DMA((count,)),
        ]

    def zcopy(self, w, way, step, blk, src):
        slot = blk * 2 + self.b
        return remote(
            src, self.weights[w][1].at[slot], self.zsend.at[w, way, step],
            self.wrecv.at[w, slot], (self.line + (1 if way == 0 else -1)) * 2 + self.b, self.t,
        )

    def xcopy(self, w, blk, b, src):
        slot = blk * 2 + b
        return remote(
            src, self.weights[w][1].at[slot], self.xsend.at[w, blk], self.wrecv.at[w, slot],
            self.line * 2 + (1 - self.b), self.t,
        )

    def local(self, w):
        return pltpu.make_async_copy(self.weights[w][0], self.weights[w][1].at[self.d], self.lsem.at[w])

    def more(self, way):
        return (self.line + 1 < self.line_count) if way == 0 else (self.line > 0)

    def start(self):
        for w in range(len(self.weights)):
            own = self.weights[w][0]
            for way in range(2):

                @pl.when(self.more(way))
                def _():
                    self.zcopy(w, way, 0, self.line, own).start()

            self.xcopy(w, self.line, self.b, own).start()
            self.local(w).start()

    def hops(self, act, sending=False):
        def hop(step, carry):
            for w in range(len(self.weights)):
                for way in range(2):
                    blk = self.line - step if way == 0 else self.line + step

                    valid = (blk >= 0) if way == 0 else (blk < self.line_count)
                    if sending:
                        valid = valid & self.more(way)

                    @pl.when(valid)
                    def _():
                        act(w, way, step, blk, self.weights[w][1].at[blk * 2 + self.b])

            return carry

        lax.fori_loop(1, self.line_count, hop, 0)

    def relay(self):
        def act(w, way, step, blk, src):
            self.zcopy(w, way, step, blk, src).wait_recv()

            @pl.when(self.more(way))
            def _():
                self.zcopy(w, way, step, blk, src).start()

            self.xcopy(w, blk, self.b, src).start()

        self.hops(act)

    def finish(self):
        for w in range(len(self.weights)):
            self.local(w).wait()
            for way in range(2):

                @pl.when(self.more(way))
                def _():
                    self.zcopy(w, way, 0, self.line, self.weights[w][0]).wait_send()

        def act(w, way, step, blk, src):
            self.zcopy(w, way, step, blk, src).wait_send()

        self.hops(act, sending=True)

        def pair(blk, carry):
            for w in range(len(self.weights)):
                own = self.weights[w][0]
                self.xcopy(w, blk, self.b, own).wait_send()
                self.xcopy(w, blk, 1 - self.b, own).wait_recv()
            return carry

        lax.fori_loop(0, self.line_count, pair, 0)


class LineReduce:
    def __init__(self, dp_count, grads, outs, buffers, xsend, xrecv, zsend, zrecv):
        n = len(grads)
        self.n, self.grads, self.outs = n, grads, outs
        self.held, self.below, self.above = buffers[:n], buffers[n : 2 * n], buffers[2 * n :]
        self.xsend, self.xrecv, self.zsend, self.zrecv = xsend, xrecv, zsend, zrecv
        self.line_count = dp_count // 2
        self.d, self.t = place()
        self.line, self.b = self.d // 2, self.d % 2

    @staticmethod
    def scratch(dp_count, blocks):
        line_count, n = dp_count // 2, len(blocks)
        return [pltpu.VMEM((line_count,) + s, BF16) for s in blocks] * 3 + [
            pltpu.SemaphoreType.DMA((n, line_count)),
            pltpu.SemaphoreType.DMA((n, line_count)),
            pltpu.SemaphoreType.DMA((n, line_count)),
            pltpu.SemaphoreType.DMA((n, 2, line_count)),
        ]

    def xcopy(self, w, target):
        return remote(
            self.grads[w].at[target * 2 + (1 - self.b)], self.held[w].at[target],
            self.xsend.at[w, target], self.xrecv.at[w, target],
            self.line * 2 + (1 - self.b), self.t,
        )

    def zcopy(self, w, way, target):
        dst = (self.below if way == 0 else self.above)[w]
        return remote(
            self.held[w].at[target], dst.at[target], self.zsend.at[w, target],
            self.zrecv.at[w, way, target],
            (self.line + (1 if way == 0 else -1)) * 2 + self.b, self.t,
        )

    def each_target(self, act):
        last = self.line_count - 1

        def step(i, carry):
            @pl.when(last - i > self.line)
            def _():
                act(0, last - i)

            @pl.when(i < self.line)
            def _():
                act(1, i)

            return carry

        lax.fori_loop(0, last, step, 0)

    def start(self):
        def send(way, target):
            for w in range(self.n):
                self.xcopy(w, target).start()

        self.each_target(send)
        send(0, self.line)

    def has(self, way):
        return (self.line > 0) if way == 0 else (self.line + 1 < self.line_count)

    def run(self):
        def reduce(way, target):
            for w in range(self.n):
                self.xcopy(w, target).wait_recv()
                dst = (self.below if way == 0 else self.above)[w]
                held, grad = self.held[w], self.grads[w]

                @pl.when(self.has(way))
                def _():
                    self.zcopy(w, way, target).wait_recv()
                    held[target] = (
                        grad[target * 2 + self.b].astype(F32)
                        + held[target].astype(F32)
                        + dst[target].astype(F32)
                    ).astype(BF16)

                @pl.when(jnp.logical_not(self.has(way)))
                def _():
                    held[target] = (
                        grad[target * 2 + self.b].astype(F32) + held[target].astype(F32)
                    ).astype(BF16)

                self.zcopy(w, way, target).start()

        self.each_target(reduce)

    def finish(self):
        for w in range(self.n):
            self.xcopy(w, self.line).wait_recv()
            out = self.outs[w]
            out[...] = self.grads[w][self.d].astype(F32) + self.held[w][self.line].astype(F32)
            for way in range(2):

                @pl.when(self.has(way))
                def _():
                    self.zcopy(w, way, self.line).wait_recv()
                    out[...] += (self.below if way == 0 else self.above)[w][self.line].astype(F32)

    def drain(self):
        def act(way, target):
            for w in range(self.n):
                self.zcopy(w, way, target).wait_send()
                self.xcopy(w, target).wait_send()

        self.each_target(act)
        for w in range(self.n):
            self.xcopy(w, self.line).wait_send()


def gather_kernel(dp_count, *refs):
    vec_ref, x_ref, og_ref, w0, w1, vec_out, attn_in, out_low, o0, o1, *scratch = refs
    enter(dp_count)
    vsum = VectorSum(dp_count, *scratch[4:10])
    vsum.start(vec_ref[...])
    weights = LineGather(dp_count, [(w0, o0), (w1, o1)], *scratch[:4])
    gather_x = TensorGather(attn_in, *scratch[10:12])
    gather_o = TensorGather(out_low, *scratch[12:14])
    weights.start()
    gather_o.start(og_ref[...])
    vsum.middle()
    vec = vsum.finish()
    vec_out[...] = vec
    normed = layer_normalize(x_ref[...], vec[0:1], vec[1:2])[0]
    gather_x.start(normed.astype(BF16))
    weights.relay()
    gather_o.forward()
    gather_x.forward()
    weights.finish()
    gather_o.finish()
    gather_x.finish()


def params(collective_id):
    return pltpu.CompilerParams(
        collective_id=collective_id, has_side_effects=True, vmem_limit_bytes=60 * 1024 * 1024
    )


def vmem(count):
    return [pl.BlockSpec(memory_space=pltpu.VMEM)] * count


def hbm(count):
    return [pl.BlockSpec(memory_space=pl.ANY)] * count


def gather_all(dp_count, vec, x, og, weights):
    rows, width = x.shape
    shape = jax.ShapeDtypeStruct
    return pl.pallas_call(
        functools.partial(gather_kernel, dp_count),
        out_shape=[
            shape(vec.shape, F32),
            shape((4, rows, width), BF16),
            shape((4, rows, width), BF16),
        ] + [shape((dp_count,) + w.shape, BF16) for w in weights],
        in_specs=vmem(5),
        out_specs=vmem(3) + hbm(2),
        scratch_shapes=LineGather.scratch(dp_count, 2)
        + VectorSum.scratch(dp_count, width)
        + TensorGather.scratch()
        + TensorGather.scratch(),
        compiler_params=params(1),
        name="gather_all",
    )(vec, x, og, *weights)


def middle_kernel(dp_count, *refs):
    part, x_ref, vec_ref, w0, w1, middle_ref, mlp_in, o0, o1, *scratch = refs
    enter(dp_count)
    scatter = TensorScatter(part, *scratch[:5])
    gather = TensorGather(mlp_in, *scratch[5:7])
    weights = LineGather(dp_count, [(w0, o0), (w1, o1)], *scratch[7:11])
    scatter.start()
    weights.start()
    scatter.middle()
    base = x_ref[...] + vec_ref[2:3]
    middle = base + scatter.finish()
    middle_ref[...] = middle
    gather.start(layer_normalize(middle, vec_ref[3:4], vec_ref[4:5])[0].astype(BF16))
    weights.relay()
    gather.forward()
    weights.finish()
    gather.finish()


def middle_exchange(dp_count, part, x, vec, weights):
    rows, width = x.shape
    shape = jax.ShapeDtypeStruct
    return pl.pallas_call(
        functools.partial(middle_kernel, dp_count),
        out_shape=[shape(x.shape, F32), shape((4, rows, width), BF16)]
        + [shape((dp_count,) + w.shape, BF16) for w in weights],
        in_specs=vmem(5),
        out_specs=vmem(2) + hbm(2),
        scratch_shapes=TensorScatter.scratch(rows, width)
        + TensorGather.scratch()
        + LineGather.scratch(dp_count, 2),
        compiler_params=params(2),
        name="middle_exchange",
    )(part, x, vec, *weights)


def put_rows(base, values):
    row = lax.broadcasted_iota(jnp.int32, base.shape, 0)
    for index, value in values:
        base = jnp.where(row == index, value, base)
    return base


def column_sum(value):
    return jnp.sum(value, axis=0, keepdims=True)


def back_kernel(dp_count, *refs):
    (part, part_out, middle_ref, run_ref, vec_ref, g0, g1,
     block_out, grad_ref, low, sums_ref, o0, o1, *scratch) = refs
    enter(dp_count)
    scatter = TensorScatter(part, *scratch[:5])
    scatter_out = TensorScatter(part_out, *scratch[5:10])
    gather = TensorGather(low, *scratch[10:12])
    line = LineReduce(dp_count, (g0, g1), (o0, o1), scratch[12:18], *scratch[18:22])
    scatter.start()
    line.start()
    scatter.middle()
    _, normed, inverse = layer_normalize(middle_ref[...], vec_ref[3:4], vec_ref[4:5])
    upstream = scatter.finish()
    grad = run_ref[...] + norm_backward_step(upstream, vec_ref[3:4], normed, inverse)
    grad_ref[...] = grad
    gather.start(grad.astype(BF16))
    scatter_out.start()
    sums_ref[...] = put_rows(
        jnp.zeros(sums_ref.shape, F32),
        [
            (2, column_sum(grad)),
            (3, column_sum(upstream * normed)),
            (4, column_sum(upstream)),
            (5, column_sum(run_ref[...])),
        ],
    )
    line.run()
    gather.forward()
    scatter_out.middle()
    line.finish()
    block_out[...] = middle_ref[...] + scatter_out.finish() + vec_ref[5:6]
    gather.finish()
    line.drain()


def back_exchange(dp_count, part, part_out, middle, run, vec, grads):
    rows, width = middle.shape
    shape = jax.ShapeDtypeStruct
    blocks = [g.shape[1:] for g in grads]
    return pl.pallas_call(
        functools.partial(back_kernel, dp_count),
        out_shape=[
            shape(middle.shape, F32),
            shape(middle.shape, F32),
            shape((4, rows, width), BF16),
            shape((VECTOR_ROWS, width), F32),
        ]
        + [shape(s, F32) for s in blocks],
        in_specs=vmem(7),
        out_specs=vmem(6),
        scratch_shapes=TensorScatter.scratch(rows, width)
        + TensorScatter.scratch(rows, width)
        + TensorGather.scratch()
        + LineReduce.scratch(dp_count, blocks),
        compiler_params=params(3),
        name="back_exchange",
    )(part, part_out, middle, run, vec, *grads)


def reduce_kernel(dp_count, *refs):
    (part_in, x_ref, mgrad_ref, vec_ref, sums_ref, g0, g1,
     input_grad, sums_out, o0, o1, *scratch) = refs
    enter(dp_count)
    line = LineReduce(dp_count, (g0, g1), (o0, o1), scratch[:6], *scratch[6:10])
    vsum = VectorSum(dp_count, *scratch[10:16])
    scatter_in = TensorScatter(part_in, *scratch[16:21])
    scatter_in.start()
    line.start()
    scatter_in.middle()
    _, normed, inverse = layer_normalize(x_ref[...], vec_ref[0:1], vec_ref[1:2])
    upstream = scatter_in.finish()
    vsum.start(
        put_rows(
            sums_ref[...], [(0, column_sum(upstream * normed)), (1, column_sum(upstream))]
        )
    )
    input_grad[...] = mgrad_ref[...] + norm_backward_step(
        upstream, vec_ref[0:1], normed, inverse
    )
    line.run()
    vsum.middle()
    line.finish()
    sums_out[...] = vsum.finish()
    line.drain()


def reduce_all(dp_count, part_in, x, mgrad, vec, sums, grads):
    rows, width = x.shape
    shape = jax.ShapeDtypeStruct
    blocks = [g.shape[1:] for g in grads]
    return pl.pallas_call(
        functools.partial(reduce_kernel, dp_count),
        out_shape=[shape(x.shape, F32), shape(vec.shape, F32)] + [shape(s, F32) for s in blocks],
        in_specs=vmem(7),
        out_specs=vmem(4),
        scratch_shapes=LineReduce.scratch(dp_count, blocks)
        + VectorSum.scratch(dp_count, width)
        + TensorScatter.scratch(rows, width),
        compiler_params=params(4),
        name="reduce_all",
    )(part_in, x, mgrad, vec, sums, *grads)


def per_device(
    dp_count,
    block_input,
    seq_begin,
    group_fill,
    attention_norm_gain,
    attention_norm_bias,
    qkv_weight,
    qv_bias,
    dense_weight,
    dense_bias,
    feedforward_norm_gain,
    feedforward_norm_bias,
    up_weight,
    up_bias,
    down_weight,
    down_bias,
    out_grad,
):
    head_dim = D // HEADS
    own_rows, width = block_input.shape
    group_rows = seq_begin.shape[0]
    dp_index, tensor_index = lax.axis_index("dp"), lax.axis_index("tensor")
    shard = dp_index * 4 + tensor_index
    norm_vectors = jnp.stack(
        [
            attention_norm_gain,
            attention_norm_bias,
            dense_bias,
            feedforward_norm_gain,
            feedforward_norm_bias,
            down_bias,
        ]
    )
    piece = norm_vectors.shape[1]
    up_piece, qv_piece = up_bias.shape[0], qv_bias.shape[0]
    vec = jnp.zeros((VECTOR_ROWS, width), F32)
    vec = lax.dynamic_update_slice(vec, norm_vectors, (0, shard * piece))
    vec = lax.dynamic_update_slice(vec, up_bias.astype(F32)[None], (6, dp_index * up_piece))
    vec = lax.dynamic_update_slice(vec, qv_bias.astype(F32)[None], (7, dp_index * qv_piece))
    row_ids = tensor_index * own_rows + jnp.arange(own_rows, dtype=jnp.int32)
    live_rows = (row_ids < group_fill[0]).astype(jnp.float32)[:, None]
    running_gradient = out_grad * live_rows
    vec, attn_in, out_low, qkv_full, dense_full = gather_all(
        dp_count,
        vec,
        block_input,
        running_gradient.astype(BF16),
        (qkv_weight, dense_weight),
    )
    attn_in = attn_in.reshape(group_rows, width)
    out_low = out_low.reshape(group_rows, width)
    qkv_full, dense_full = (w.reshape(-1, w.shape[-1]) for w in (qkv_full, dense_full))
    local_heads = qkv_full.shape[1] // (3 * head_dim)
    slopes = head_slopes((tensor_index * local_heads).astype(jnp.float32), local_heads)
    projected = jnp.dot(attn_in, qkv_full, preferred_element_type=jnp.float32).reshape(
        group_rows, local_heads, 3, head_dim
    )
    bias_pair = vec[7, : 2 * local_heads * head_dim].reshape(local_heads, 2, head_dim)
    bias_full = jnp.stack(
        [bias_pair[:, 0], jnp.zeros_like(bias_pair[:, 0]), bias_pair[:, 1]], axis=1
    )
    qkv_low = (projected + bias_full).astype(jnp.bfloat16)
    queries = qkv_low[:, :, 0]
    key_all = qkv_low[:, :, 1]
    values = qkv_low[:, :, 2]
    context, log_total = attention_forward(queries, key_all, values, slopes, seq_begin)
    context_flat = context.reshape(group_rows, local_heads * head_dim)
    attn_part = jnp.dot(context_flat, dense_full, preferred_element_type=jnp.float32).astype(BF16)
    residual_middle, mlp_in, up_full, down_full = middle_exchange(
        dp_count,
        attn_part.reshape(4, own_rows, width),
        block_input,
        vec,
        (up_weight, down_weight),
    )
    up_full, down_full = (w.reshape(-1, w.shape[-1]) for w in (up_full, down_full))
    mlp_in = mlp_in.reshape(group_rows, width)
    pre_act = jnp.dot(mlp_in, up_full, preferred_element_type=jnp.float32) + vec[6]
    act_value, act_back = jax.vjp(gelu_tanh, pre_act)
    activated = act_value.astype(jnp.bfloat16)
    act_grad = lax.dot_general(
        out_low, down_full, CONTRACT_COLS, preferred_element_type=jnp.float32
    )
    pre_grad = act_back(act_grad)[0].astype(jnp.bfloat16)
    mlp_in_part = lax.dot_general(
        pre_grad, up_full, CONTRACT_COLS, preferred_element_type=jnp.float32
    ).astype(BF16)
    mlp_part = jnp.dot(activated, down_full, preferred_element_type=jnp.float32).astype(BF16)
    down_grad = lax.dot_general(
        activated, out_low, CONTRACT_ROWS, preferred_element_type=jnp.float32
    )
    up_grad = lax.dot_general(mlp_in, pre_grad, CONTRACT_ROWS, preferred_element_type=jnp.float32)
    up_shift_grad = jnp.sum(pre_grad.astype(jnp.float32), axis=0)
    block_out, residual_middle_gradient, middle_low, sums, up_out, down_out = back_exchange(
        dp_count,
        mlp_in_part.reshape(4, own_rows, width),
        mlp_part.reshape(4, own_rows, width),
        residual_middle,
        running_gradient,
        vec,
        tuple(g.astype(BF16).reshape(dp_count, -1, g.shape[-1]) for g in (up_grad, down_grad)),
    )
    middle_low = middle_low.reshape(group_rows, width)
    dense_grad = lax.dot_general(
        context_flat, middle_low, CONTRACT_ROWS, preferred_element_type=jnp.float32
    )
    context_grad = lax.dot_general(
        middle_low, dense_full, CONTRACT_COLS, preferred_element_type=jnp.float32
    )
    context_grad = context_grad.astype(jnp.bfloat16).reshape(group_rows, local_heads, head_dim)
    qkv_grad = attention_backward(
        queries, key_all, values, slopes, seq_begin, log_total, context, context_grad
    )
    qkv_grad_flat = qkv_grad.reshape(group_rows, 3 * local_heads * head_dim)
    qkv_grad_sum = lax.dot_general(
        attn_in, qkv_grad_flat, CONTRACT_ROWS, preferred_element_type=jnp.float32
    )
    summed = jnp.sum(qkv_grad.astype(jnp.float32), axis=0)
    qv_grad = jnp.stack([summed[:, 0], summed[:, 2]], axis=1).reshape(2 * local_heads * head_dim)
    attn_in_part = lax.dot_general(
        qkv_grad_flat, qkv_full, CONTRACT_COLS, preferred_element_type=jnp.float32
    ).astype(BF16)
    sums = lax.dynamic_update_slice(sums, up_shift_grad[None], (6, 0))
    sums = lax.dynamic_update_slice(sums, qv_grad[None], (7, 0))
    grads = tuple(
        g.astype(BF16).reshape(dp_count, -1, g.shape[-1])
        for g in (qkv_grad_sum, dense_grad)
    )
    block_input_gradient, sums, qkv_out, dense_out = reduce_all(
        dp_count,
        attn_in_part.reshape(4, own_rows, width),
        block_input,
        residual_middle_gradient,
        vec,
        sums,
        grads,
    )
    vectors = lax.dynamic_slice(sums, (0, shard * piece), (6, piece))
    up_shift_out = lax.dynamic_slice(sums, (6, dp_index * up_piece), (1, up_piece))[0]
    qv_out = lax.dynamic_slice(sums, (7, dp_index * qv_piece), (1, qv_piece))[0]
    return (
        block_out,
        block_input_gradient,
        vectors[0],
        vectors[1],
        qkv_out,
        qv_out,
        dense_out,
        vectors[2],
        vectors[3],
        vectors[4],
        up_out,
        up_shift_out,
        down_out,
        vectors[5],
    )


def solution(mesh):
    return jax.shard_map(
        functools.partial(per_device, mesh.shape["dp"]),
        mesh=mesh,
        in_specs=(
            P(("dp", "tensor"), None),
            P("dp"),
            P("dp"),
            P(("dp", "tensor")),
            P(("dp", "tensor")),
            P("dp", "tensor"),
            P(("tensor", "dp")),
            P(("tensor", "dp"), None),
            P(("dp", "tensor")),
            P(("dp", "tensor")),
            P(("dp", "tensor")),
            P("dp", "tensor"),
            P(("tensor", "dp")),
            P(("tensor", "dp"), None),
            P(("dp", "tensor")),
            P(("dp", "tensor"), None),
        ),
        out_specs=(
            P(("dp", "tensor"), None),
            P(("dp", "tensor"), None),
            P(("dp", "tensor")),
            P(("dp", "tensor")),
            P("dp", "tensor"),
            P(("tensor", "dp")),
            P(("tensor", "dp"), None),
            P(("dp", "tensor")),
            P(("dp", "tensor")),
            P(("dp", "tensor")),
            P("dp", "tensor"),
            P(("tensor", "dp")),
            P(("tensor", "dp"), None),
            P(("dp", "tensor")),
        ),
        check_vma=False,
    )
```

```python
import functools
import math

import jax
import jax.numpy as jnp
from jax import lax
from jax.experimental import pallas as pl
from jax.experimental.pallas import tpu as pltpu
from jax.sharding import PartitionSpec as P

D = 1024
HEADS = 16


EPSILON = 1e-05
MASKED_SCORE = -1e30
CONTRACT_ROWS = (((0,), (0,)), ((), ()))
CONTRACT_COLS = (((1,), (1,)), ((), ()))


def layer_normalize(hidden_row_count, norm_gain, norm_shift):
    row_mean = jnp.mean(hidden_row_count, axis=-1, keepdims=True)
    centred = hidden_row_count - row_mean
    inv_std = lax.rsqrt(jnp.mean(centred * centred, axis=-1, keepdims=True) + EPSILON)
    normed = centred * inv_std
    return (normed * norm_gain + norm_shift, normed, inv_std)


def norm_backward_step(upstream, norm_gain, normed, inv_std):
    scaled = upstream * norm_gain
    return inv_std * (
        scaled
        - jnp.mean(scaled, axis=-1, keepdims=True)
        - normed * jnp.mean(scaled * normed, axis=-1, keepdims=True)
    )


def gelu_tanh(values_in):
    return jax.nn.gelu(values_in, approximate=True)


def head_slopes(first_head, head_count):
    heads_idx = first_head + jnp.arange(head_count).astype(jnp.float32)
    return jnp.exp2(-8.0 * (heads_idx + 1.0) / HEADS)


def masked_scores(query_blk, key_all, slopes, begin_blk):
    row_count = query_blk.shape[0]
    key_count = key_all.shape[0]
    query_pos = jnp.arange(row_count, dtype=jnp.int32)
    key_pos = jnp.arange(key_count, dtype=jnp.int32)
    score_scale = 1.0 / math.sqrt(query_blk.shape[-1])
    logits = (
        jnp.einsum("qhd,khd->hqk", query_blk, key_all, preferred_element_type=jnp.float32)
        * score_scale
    )
    offset = (key_pos[None, :] - query_pos[:, None]).astype(jnp.float32)
    logits = logits + slopes[:, None, None] * offset[None, :, :]
    allowed = (key_pos[None, :] >= begin_blk[:, None]) & (key_pos[None, :] <= query_pos[:, None])
    return jnp.where(allowed[None, :, :], logits, MASKED_SCORE)


def attention_forward(queries, key_all, values, slopes, begins):
    scores = masked_scores(queries, key_all, slopes, begins)
    row_top = jnp.max(scores, axis=-1)
    log_total = row_top + jnp.log(jnp.sum(jnp.exp(scores - row_top[..., None]), axis=-1))
    attn_probs = jnp.exp(scores - log_total[..., None]).astype(jnp.bfloat16)
    pieces = jnp.einsum(
        "hqk,khd->qhd", attn_probs, values, preferred_element_type=jnp.float32
    ).astype(jnp.bfloat16)
    return (pieces, log_total)


def attention_backward(queries, key_all, values, slopes, begins, log_total, context, context_grad):
    total_rows = queries.shape[0]
    block_rows = min(512, total_rows)
    score_scale = 1.0 / math.sqrt(queries.shape[-1])
    scores = masked_scores(queries, key_all, slopes, begins)
    attn_probs = jnp.exp(scores - log_total[:, 0:block_rows, None])
    row_delta = jnp.sum(context_grad.astype(jnp.float32) * context.astype(jnp.float32), axis=-1)
    value_grad = jnp.einsum(
        "hqk,qhd->khd",
        attn_probs.astype(jnp.bfloat16),
        context_grad,
        preferred_element_type=jnp.float32,
    )
    prob_grad = jnp.einsum("qhd,khd->hqk", context_grad, values, preferred_element_type=jnp.float32)
    score_grad = (attn_probs * (prob_grad - jnp.transpose(row_delta)[:, :, None])).astype(
        jnp.bfloat16
    )
    query_parts = (
        jnp.einsum("hqk,khd->qhd", score_grad, key_all, preferred_element_type=jnp.float32)
        * score_scale
    )
    key_grad = (
        jnp.einsum("hqk,qhd->khd", score_grad, queries, preferred_element_type=jnp.float32)
        * score_scale
    )
    return jnp.stack([query_parts, key_grad, value_grad], axis=2).astype(jnp.bfloat16)

MESH = pl.DeviceIdType.MESH
VECTOR_ROWS = 8
BF16 = jnp.bfloat16
F32 = jnp.float32


def place():
    return lax.axis_index("dp"), lax.axis_index("tensor")


def tensor_peers(t):
    h, c = t // 2, t % 2
    core = h * 2 + (1 - c)
    across = (1 - h) * 2 + c
    diagonal = (1 - h) * 2 + (1 - c)
    return core, across, diagonal


def enter(dp_count):
    d, t = place()
    barrier = pltpu.get_barrier_semaphore()
    for j in range(1, 4):
        pl.semaphore_signal(
            barrier, inc=1, device_id=(d, lax.rem(t + j, 4)), device_id_type=MESH
        )
    if dp_count == 1:
        pl.semaphore_wait(barrier, 3)
        return

    def greet(j, carry):
        pl.semaphore_signal(
            barrier, inc=1, device_id=(lax.rem(d + j, dp_count), t), device_id_type=MESH
        )
        return carry

    lax.fori_loop(1, dp_count, greet, 0)
    pl.semaphore_wait(barrier, 3 + dp_count - 1)


def remote(src, dst, send, recv, d, t):
    return pltpu.make_async_remote_copy(
        src_ref=src, dst_ref=dst, send_sem=send, recv_sem=recv, device_id=(d, t), device_id_type=MESH
    )


class VectorSum:
    def __init__(self, dp_count, dbuf, tbuf, dsend, drecv, tsend, trecv):
        self.dp_count = dp_count
        self.dbuf, self.tbuf = dbuf, tbuf
        self.dsend, self.drecv, self.tsend, self.trecv = dsend, drecv, tsend, trecv

    @staticmethod
    def scratch(dp_count, width):
        return [
            pltpu.VMEM((dp_count, VECTOR_ROWS, width), F32),
            pltpu.VMEM((4, VECTOR_ROWS, width), F32),
            pltpu.SemaphoreType.DMA((dp_count,)),
            pltpu.SemaphoreType.DMA((dp_count,)),
            pltpu.SemaphoreType.DMA((4,)),
            pltpu.SemaphoreType.DMA((4,)),
        ]

    def dcopy(self, j):
        d, t = place()
        return remote(
            self.dbuf.at[0], self.dbuf.at[j], self.dsend.at[j], self.drecv.at[j],
            lax.rem(d + j, self.dp_count), t,
        )

    def tcopy(self, j):
        d, t = place()
        return remote(
            self.tbuf.at[0], self.tbuf.at[j], self.tsend.at[j], self.trecv.at[j],
            d, lax.rem(t + j, 4),
        )

    def start(self, value):
        self.dbuf[0] = value

        def go(j, carry):
            self.dcopy(j).start()
            return carry

        lax.fori_loop(1, self.dp_count, go, 0)

    def middle(self):
        def wait(j, carry):
            self.dcopy(j).wait()
            return carry

        lax.fori_loop(1, self.dp_count, wait, 0)
        self.tbuf[0] = jnp.sum(self.dbuf[...], axis=0)
        for j in range(1, 4):
            self.tcopy(j).start()

    def finish(self):
        for j in range(1, 4):
            self.tcopy(j).wait()
        own = self.tbuf[0]
        total = own + self.tbuf[1] + self.tbuf[2] + self.tbuf[3]
        row = lax.broadcasted_iota(jnp.int32, own.shape, 0)
        return jnp.where(row < 6, total, own)


class TensorGather:
    def __init__(self, buf, send, recv):
        self.buf, self.send, self.recv = buf, send, recv
        d, t = place()
        core, across, diagonal = tensor_peers(t)
        half = buf.shape[1] // 2
        part = [pl.ds(k * half, half) for k in range(2)]
        at = lambda s, k: buf.at[s, part[k]]
        self.to_across = [
            remote(at(t, k), at(t, k), send.at[k], recv.at[k], d, across) for k in range(2)
        ]
        self.to_core = [
            remote(at(t, k), at(t, k), send.at[2 + k], recv.at[2 + k], d, core) for k in range(2)
        ]
        self.relay = [
            remote(at(across, k), at(across, k), send.at[4 + k], recv.at[4 + k], d, core)
            for k in range(2)
        ]

    @staticmethod
    def scratch():
        return [pltpu.SemaphoreType.DMA((6,)), pltpu.SemaphoreType.DMA((6,))]

    def start(self, value):
        _, t = place()
        self.buf[t] = value
        for c in self.to_across + self.to_core:
            c.start()

    def forward(self):
        for k in range(2):
            self.to_across[k].wait_recv()
            self.relay[k].start()

    def finish(self):
        for c in self.to_across:
            c.wait_send()
        for c in self.to_core + self.relay:
            c.wait()


class TensorScatter:
    def __init__(self, part, near, far, out, send, recv):
        self.part, self.near, self.far, self.out = part, near, far, out
        d, t = place()
        core, across, diagonal = tensor_peers(t)
        half = part.shape[1] // 2
        self.rows = [pl.ds(k * half, half) for k in range(2)]
        r = self.rows
        self.first = [
            remote(part.at[diagonal, r[k]], near.at[1, r[k]], send.at[k], recv.at[k], d, core)
            for k in range(2)
        ]
        self.own = [
            remote(part.at[core, r[k]], near.at[0, r[k]], send.at[2 + k], recv.at[2 + k], d, core)
            for k in range(2)
        ]
        self.second = [
            remote(out.at[r[k]], far.at[r[k]], send.at[4 + k], recv.at[4 + k], d, across)
            for k in range(2)
        ]

    @staticmethod
    def scratch(rows, width):
        return [
            pltpu.VMEM((2, rows, width), BF16),
            pltpu.VMEM((rows, width), BF16),
            pltpu.VMEM((rows, width), BF16),
            pltpu.SemaphoreType.DMA((6,)),
            pltpu.SemaphoreType.DMA((6,)),
        ]

    def start(self):
        for c in self.first + self.own:
            c.start()

    def middle(self):
        _, t = place()
        _, across, _ = tensor_peers(t)
        for k in range(2):
            self.first[k].wait_recv()
            r = self.rows[k]
            self.out[r] = (
                self.part[across, r].astype(F32) + self.near[1, r].astype(F32)
            ).astype(BF16)
            self.second[k].start()

    def finish(self):
        _, t = place()
        for c in self.first:
            c.wait_send()
        for c in self.own + self.second:
            c.wait()
        return (
            self.part[t].astype(F32) + self.near[0].astype(F32) + self.far[...].astype(F32)
        )


class LineGather:
    def __init__(self, dp_count, weights, zsend, xsend, wrecv, lsem):
        self.weights, self.line_count = weights, dp_count // 2
        self.zsend, self.xsend, self.wrecv, self.lsem = zsend, xsend, wrecv, lsem
        self.d, self.t = place()
        self.line, self.b = self.d // 2, self.d % 2

    @staticmethod
    def scratch(dp_count, count):
        return [
            pltpu.SemaphoreType.DMA((count, 2, dp_count // 2)),
            pltpu.SemaphoreType.DMA((count, dp_count // 2)),
            pltpu.SemaphoreType.DMA((count, dp_count)),
            pltpu.SemaphoreType.DMA((count,)),
        ]

    def zcopy(self, w, way, step, blk, src):
        slot = blk * 2 + self.b
        return remote(
            src, self.weights[w][1].at[slot], self.zsend.at[w, way, step],
            self.wrecv.at[w, slot], (self.line + (1 if way == 0 else -1)) * 2 + self.b, self.t,
        )

    def xcopy(self, w, blk, b, src):
        slot = blk * 2 + b
        return remote(
            src, self.weights[w][1].at[slot], self.xsend.at[w, blk], self.wrecv.at[w, slot],
            self.line * 2 + (1 - self.b), self.t,
        )

    def local(self, w):
        return pltpu.make_async_copy(self.weights[w][0], self.weights[w][1].at[self.d], self.lsem.at[w])

    def more(self, way):
        return (self.line + 1 < self.line_count) if way == 0 else (self.line > 0)

    def start(self):
        for w in range(len(self.weights)):
            own = self.weights[w][0]
            for way in range(2):

                @pl.when(self.more(way))
                def _():
                    self.zcopy(w, way, 0, self.line, own).start()

            self.xcopy(w, self.line, self.b, own).start()
            self.local(w).start()

    def hops(self, act, first, last, sending=False):
        def hop(step, carry):
            for w in range(len(self.weights)):
                for way in range(2):
                    blk = self.line - step if way == 0 else self.line + step

                    valid = (blk >= 0) if way == 0 else (blk < self.line_count)
                    if sending:
                        valid = valid & self.more(way)

                    @pl.when(valid)
                    def _():
                        act(w, way, step, blk, self.weights[w][1].at[blk * 2 + self.b])

            return carry

        if first < last:
            lax.fori_loop(first, last, hop, 0)

    def relay(self, first=1, last=None):
        last = self.line_count if last is None else min(last, self.line_count)

        def act(w, way, step, blk, src):
            self.zcopy(w, way, step, blk, src).wait_recv()

            @pl.when(self.more(way))
            def _():
                self.zcopy(w, way, step, blk, src).start()

            self.xcopy(w, blk, self.b, src).start()

        self.hops(act, first, last)

    def finish(self):
        for w in range(len(self.weights)):
            self.local(w).wait()
            for way in range(2):

                @pl.when(self.more(way))
                def _():
                    self.zcopy(w, way, 0, self.line, self.weights[w][0]).wait_send()

        def act(w, way, step, blk, src):
            self.zcopy(w, way, step, blk, src).wait_send()

        self.hops(act, 1, self.line_count, sending=True)

        def pair(blk, carry):
            for w in range(len(self.weights)):
                own = self.weights[w][0]
                self.xcopy(w, blk, self.b, own).wait_send()
                self.xcopy(w, blk, 1 - self.b, own).wait_recv()
            return carry

        lax.fori_loop(0, self.line_count, pair, 0)


class LineReduce:
    def __init__(self, dp_count, grads, outs, buffers, xsend, xrecv, zsend, zrecv):
        n = len(grads)
        self.n, self.grads, self.outs = n, grads, outs
        self.held, self.below, self.above = buffers[:n], buffers[n : 2 * n], buffers[2 * n :]
        self.xsend, self.xrecv, self.zsend, self.zrecv = xsend, xrecv, zsend, zrecv
        self.line_count = dp_count // 2
        self.d, self.t = place()
        self.line, self.b = self.d // 2, self.d % 2

    @staticmethod
    def scratch(dp_count, blocks):
        line_count, n = dp_count // 2, len(blocks)
        return [pltpu.VMEM((line_count,) + s, BF16) for s in blocks] * 3 + [
            pltpu.SemaphoreType.DMA((n, line_count)),
            pltpu.SemaphoreType.DMA((n, line_count)),
            pltpu.SemaphoreType.DMA((n, line_count)),
            pltpu.SemaphoreType.DMA((n, 2, line_count)),
        ]

    def xcopy(self, w, target):
        return remote(
            self.grads[w].at[target * 2 + (1 - self.b)], self.held[w].at[target],
            self.xsend.at[w, target], self.xrecv.at[w, target],
            self.line * 2 + (1 - self.b), self.t,
        )

    def zcopy(self, w, way, target):
        dst = (self.below if way == 0 else self.above)[w]
        return remote(
            self.held[w].at[target], dst.at[target], self.zsend.at[w, target],
            self.zrecv.at[w, way, target],
            (self.line + (1 if way == 0 else -1)) * 2 + self.b, self.t,
        )

    def each_target(self, act, first=0, stop=None):
        last = self.line_count - 1
        stop = last if stop is None else min(stop, last)

        def step(i, carry):
            @pl.when(last - i > self.line)
            def _():
                act(0, last - i)

            @pl.when(i < self.line)
            def _():
                act(1, i)

            return carry

        if first < stop:
            lax.fori_loop(first, stop, step, 0)

    def start(self):
        def send(way, target):
            for w in range(self.n):
                self.xcopy(w, target).start()

        self.each_target(send)
        send(0, self.line)

    def has(self, way):
        return (self.line > 0) if way == 0 else (self.line + 1 < self.line_count)

    def run(self, first=0, stop=None):
        def reduce(way, target):
            for w in range(self.n):
                self.xcopy(w, target).wait_recv()
                dst = (self.below if way == 0 else self.above)[w]
                held, grad = self.held[w], self.grads[w]

                @pl.when(self.has(way))
                def _():
                    self.zcopy(w, way, target).wait_recv()
                    held[target] = (
                        grad[target * 2 + self.b].astype(F32)
                        + held[target].astype(F32)
                        + dst[target].astype(F32)
                    ).astype(BF16)

                @pl.when(jnp.logical_not(self.has(way)))
                def _():
                    held[target] = (
                        grad[target * 2 + self.b].astype(F32) + held[target].astype(F32)
                    ).astype(BF16)

                self.zcopy(w, way, target).start()

        self.each_target(reduce, first, stop)

    def finish(self):
        for w in range(self.n):
            self.xcopy(w, self.line).wait_recv()
            out = self.outs[w]
            out[...] = self.grads[w][self.d].astype(F32) + self.held[w][self.line].astype(F32)
            for way in range(2):

                @pl.when(self.has(way))
                def _():
                    self.zcopy(w, way, self.line).wait_recv()
                    out[...] += (self.below if way == 0 else self.above)[w][self.line].astype(F32)

    def drain(self):
        def act(way, target):
            for w in range(self.n):
                self.zcopy(w, way, target).wait_send()
                self.xcopy(w, target).wait_send()

        self.each_target(act)
        for w in range(self.n):
            self.xcopy(w, self.line).wait_send()


def gather_kernel(dp_count, *refs):
    vec_ref, x_ref, og_ref, w0, w1, vec_out, attn_in, out_low, o0, o1, *scratch = refs
    enter(dp_count)
    vsum = VectorSum(dp_count, *scratch[4:10])
    vsum.start(vec_ref[...])
    weights = LineGather(dp_count, [(w0, o0), (w1, o1)], *scratch[:4])
    gather_x = TensorGather(attn_in, *scratch[10:12])
    gather_o = TensorGather(out_low, *scratch[12:14])
    weights.start()
    gather_o.start(og_ref[...])
    vsum.middle()
    weights.relay(1, 2)
    vec = vsum.finish()
    vec_out[...] = vec
    normed = layer_normalize(x_ref[...], vec[0:1], vec[1:2])[0]
    gather_x.start(normed.astype(BF16))
    weights.relay(2)
    gather_o.forward()
    gather_x.forward()
    weights.finish()
    gather_o.finish()
    gather_x.finish()


def params(collective_id):
    return pltpu.CompilerParams(
        collective_id=collective_id, has_side_effects=True, vmem_limit_bytes=60 * 1024 * 1024
    )


def vmem(count):
    return [pl.BlockSpec(memory_space=pltpu.VMEM)] * count


def hbm(count):
    return [pl.BlockSpec(memory_space=pl.ANY)] * count


def gather_all(dp_count, vec, x, og, weights):
    rows, width = x.shape
    shape = jax.ShapeDtypeStruct
    return pl.pallas_call(
        functools.partial(gather_kernel, dp_count),
        out_shape=[
            shape(vec.shape, F32),
            shape((4, rows, width), BF16),
            shape((4, rows, width), BF16),
        ] + [shape((dp_count,) + w.shape, BF16) for w in weights],
        in_specs=vmem(5),
        out_specs=vmem(3) + hbm(2),
        scratch_shapes=LineGather.scratch(dp_count, 2)
        + VectorSum.scratch(dp_count, width)
        + TensorGather.scratch()
        + TensorGather.scratch(),
        compiler_params=params(1),
        name="gather_all",
    )(vec, x, og, *weights)


def middle_kernel(dp_count, *refs):
    part, x_ref, vec_ref, w0, w1, middle_ref, mlp_in, o0, o1, *scratch = refs
    enter(dp_count)
    scatter = TensorScatter(part, *scratch[:5])
    gather = TensorGather(mlp_in, *scratch[5:7])
    weights = LineGather(dp_count, [(w0, o0), (w1, o1)], *scratch[7:11])
    scatter.start()
    weights.start()
    scatter.middle()
    base = x_ref[...] + vec_ref[2:3]
    middle = base + scatter.finish()
    middle_ref[...] = middle
    gather.start(layer_normalize(middle, vec_ref[3:4], vec_ref[4:5])[0].astype(BF16))
    weights.relay()
    gather.forward()
    weights.finish()
    gather.finish()


def middle_exchange(dp_count, part, x, vec, weights):
    rows, width = x.shape
    shape = jax.ShapeDtypeStruct
    return pl.pallas_call(
        functools.partial(middle_kernel, dp_count),
        out_shape=[shape(x.shape, F32), shape((4, rows, width), BF16)]
        + [shape((dp_count,) + w.shape, BF16) for w in weights],
        in_specs=vmem(5),
        out_specs=vmem(2) + hbm(2),
        scratch_shapes=TensorScatter.scratch(rows, width)
        + TensorGather.scratch()
        + LineGather.scratch(dp_count, 2),
        compiler_params=params(2),
        name="middle_exchange",
    )(part, x, vec, *weights)


def put_rows(base, values):
    row = lax.broadcasted_iota(jnp.int32, base.shape, 0)
    for index, value in values:
        base = jnp.where(row == index, value, base)
    return base


def column_sum(value):
    return jnp.sum(value, axis=0, keepdims=True)


def back_kernel(dp_count, *refs):
    (part, part_out, middle_ref, run_ref, vec_ref, g0, g1,
     block_out, grad_ref, low, sums_ref, o0, o1, *scratch) = refs
    enter(dp_count)
    scatter = TensorScatter(part, *scratch[:5])
    scatter_out = TensorScatter(part_out, *scratch[5:10])
    gather = TensorGather(low, *scratch[10:12])
    line = LineReduce(dp_count, (g0, g1), (o0, o1), scratch[12:18], *scratch[18:22])
    scatter.start()
    line.start()
    scatter.middle()
    line.run(0, 1)
    _, normed, inverse = layer_normalize(middle_ref[...], vec_ref[3:4], vec_ref[4:5])
    upstream = scatter.finish()
    grad = run_ref[...] + norm_backward_step(upstream, vec_ref[3:4], normed, inverse)
    grad_ref[...] = grad
    gather.start(grad.astype(BF16))
    scatter_out.start()
    sums_ref[...] = put_rows(
        jnp.zeros(sums_ref.shape, F32),
        [
            (2, column_sum(grad)),
            (3, column_sum(upstream * normed)),
            (4, column_sum(upstream)),
            (5, column_sum(run_ref[...])),
        ],
    )
    line.run(1, 2)
    gather.forward()
    scatter_out.middle()
    line.run(2)
    line.finish()
    block_out[...] = middle_ref[...] + scatter_out.finish() + vec_ref[5:6]
    gather.finish()
    line.drain()


def back_exchange(dp_count, part, part_out, middle, run, vec, grads):
    rows, width = middle.shape
    shape = jax.ShapeDtypeStruct
    blocks = [g.shape[1:] for g in grads]
    return pl.pallas_call(
        functools.partial(back_kernel, dp_count),
        out_shape=[
            shape(middle.shape, F32),
            shape(middle.shape, F32),
            shape((4, rows, width), BF16),
            shape((VECTOR_ROWS, width), F32),
        ]
        + [shape(s, F32) for s in blocks],
        in_specs=vmem(7),
        out_specs=vmem(6),
        scratch_shapes=TensorScatter.scratch(rows, width)
        + TensorScatter.scratch(rows, width)
        + TensorGather.scratch()
        + LineReduce.scratch(dp_count, blocks),
        compiler_params=params(3),
        name="back_exchange",
    )(part, part_out, middle, run, vec, *grads)


def reduce_kernel(dp_count, *refs):
    (part_in, x_ref, mgrad_ref, vec_ref, sums_ref, g0, g1,
     input_grad, sums_out, o0, o1, *scratch) = refs
    enter(dp_count)
    line = LineReduce(dp_count, (g0, g1), (o0, o1), scratch[:6], *scratch[6:10])
    vsum = VectorSum(dp_count, *scratch[10:16])
    scatter_in = TensorScatter(part_in, *scratch[16:21])
    scatter_in.start()
    line.start()
    scatter_in.middle()
    line.run(0, 1)
    _, normed, inverse = layer_normalize(x_ref[...], vec_ref[0:1], vec_ref[1:2])
    upstream = scatter_in.finish()
    vsum.start(
        put_rows(
            sums_ref[...], [(0, column_sum(upstream * normed)), (1, column_sum(upstream))]
        )
    )
    input_grad[...] = mgrad_ref[...] + norm_backward_step(
        upstream, vec_ref[0:1], normed, inverse
    )
    line.run(1, 2)
    vsum.middle()
    line.run(2)
    line.finish()
    sums_out[...] = vsum.finish()
    line.drain()


def reduce_all(dp_count, part_in, x, mgrad, vec, sums, grads):
    rows, width = x.shape
    shape = jax.ShapeDtypeStruct
    blocks = [g.shape[1:] for g in grads]
    return pl.pallas_call(
        functools.partial(reduce_kernel, dp_count),
        out_shape=[shape(x.shape, F32), shape(vec.shape, F32)] + [shape(s, F32) for s in blocks],
        in_specs=vmem(7),
        out_specs=vmem(4),
        scratch_shapes=LineReduce.scratch(dp_count, blocks)
        + VectorSum.scratch(dp_count, width)
        + TensorScatter.scratch(rows, width),
        compiler_params=params(4),
        name="reduce_all",
    )(part_in, x, mgrad, vec, sums, *grads)


def per_device(
    dp_count,
    block_input,
    seq_begin,
    group_fill,
    attention_norm_gain,
    attention_norm_bias,
    qkv_weight,
    qv_bias,
    dense_weight,
    dense_bias,
    feedforward_norm_gain,
    feedforward_norm_bias,
    up_weight,
    up_bias,
    down_weight,
    down_bias,
    out_grad,
):
    head_dim = D // HEADS
    own_rows, width = block_input.shape
    group_rows = seq_begin.shape[0]
    dp_index, tensor_index = lax.axis_index("dp"), lax.axis_index("tensor")
    shard = dp_index * 4 + tensor_index
    norm_vectors = jnp.stack(
        [
            attention_norm_gain,
            attention_norm_bias,
            dense_bias,
            feedforward_norm_gain,
            feedforward_norm_bias,
            down_bias,
        ]
    )
    piece = norm_vectors.shape[1]
    up_piece, qv_piece = up_bias.shape[0], qv_bias.shape[0]
    vec = jnp.zeros((VECTOR_ROWS, width), F32)
    vec = lax.dynamic_update_slice(vec, norm_vectors, (0, shard * piece))
    vec = lax.dynamic_update_slice(vec, up_bias.astype(F32)[None], (6, dp_index * up_piece))
    vec = lax.dynamic_update_slice(vec, qv_bias.astype(F32)[None], (7, dp_index * qv_piece))
    row_ids = tensor_index * own_rows + jnp.arange(own_rows, dtype=jnp.int32)
    live_rows = (row_ids < group_fill[0]).astype(jnp.float32)[:, None]
    running_gradient = out_grad * live_rows
    vec, attn_in, out_low, qkv_full, dense_full = gather_all(
        dp_count,
        vec,
        block_input,
        running_gradient.astype(BF16),
        (qkv_weight, dense_weight),
    )
    attn_in = attn_in.reshape(group_rows, width)
    out_low = out_low.reshape(group_rows, width)
    qkv_full, dense_full = (w.reshape(-1, w.shape[-1]) for w in (qkv_full, dense_full))
    local_heads = qkv_full.shape[1] // (3 * head_dim)
    slopes = head_slopes((tensor_index * local_heads).astype(jnp.float32), local_heads)
    projected = jnp.dot(attn_in, qkv_full, preferred_element_type=jnp.float32).reshape(
        group_rows, local_heads, 3, head_dim
    )
    bias_pair = vec[7, : 2 * local_heads * head_dim].reshape(local_heads, 2, head_dim)
    bias_full = jnp.stack(
        [bias_pair[:, 0], jnp.zeros_like(bias_pair[:, 0]), bias_pair[:, 1]], axis=1
    )
    qkv_low = (projected + bias_full).astype(jnp.bfloat16)
    queries = qkv_low[:, :, 0]
    key_all = qkv_low[:, :, 1]
    values = qkv_low[:, :, 2]
    context, log_total = attention_forward(queries, key_all, values, slopes, seq_begin)
    context_flat = context.reshape(group_rows, local_heads * head_dim)
    attn_part = jnp.dot(context_flat, dense_full, preferred_element_type=jnp.float32).astype(BF16)
    residual_middle, mlp_in, up_full, down_full = middle_exchange(
        dp_count,
        attn_part.reshape(4, own_rows, width),
        block_input,
        vec,
        (up_weight, down_weight),
    )
    up_full, down_full = (w.reshape(-1, w.shape[-1]) for w in (up_full, down_full))
    mlp_in = mlp_in.reshape(group_rows, width)
    pre_act = jnp.dot(mlp_in, up_full, preferred_element_type=jnp.float32) + vec[6]
    act_value, act_back = jax.vjp(gelu_tanh, pre_act)
    activated = act_value.astype(jnp.bfloat16)
    act_grad = lax.dot_general(
        out_low, down_full, CONTRACT_COLS, preferred_element_type=jnp.float32
    )
    pre_grad = act_back(act_grad)[0].astype(jnp.bfloat16)
    mlp_in_part = lax.dot_general(
        pre_grad, up_full, CONTRACT_COLS, preferred_element_type=jnp.float32
    ).astype(BF16)
    mlp_part = jnp.dot(activated, down_full, preferred_element_type=jnp.float32).astype(BF16)
    down_grad = lax.dot_general(
        activated, out_low, CONTRACT_ROWS, preferred_element_type=jnp.float32
    )
    up_grad = lax.dot_general(mlp_in, pre_grad, CONTRACT_ROWS, preferred_element_type=jnp.float32)
    up_shift_grad = jnp.sum(pre_grad.astype(jnp.float32), axis=0)
    block_out, residual_middle_gradient, middle_low, sums, up_out, down_out = back_exchange(
        dp_count,
        mlp_in_part.reshape(4, own_rows, width),
        mlp_part.reshape(4, own_rows, width),
        residual_middle,
        running_gradient,
        vec,
        tuple(g.astype(BF16).reshape(dp_count, -1, g.shape[-1]) for g in (up_grad, down_grad)),
    )
    middle_low = middle_low.reshape(group_rows, width)
    dense_grad = lax.dot_general(
        context_flat, middle_low, CONTRACT_ROWS, preferred_element_type=jnp.float32
    )
    context_grad = lax.dot_general(
        middle_low, dense_full, CONTRACT_COLS, preferred_element_type=jnp.float32
    )
    context_grad = context_grad.astype(jnp.bfloat16).reshape(group_rows, local_heads, head_dim)
    qkv_grad = attention_backward(
        queries, key_all, values, slopes, seq_begin, log_total, context, context_grad
    )
    qkv_grad_flat = qkv_grad.reshape(group_rows, 3 * local_heads * head_dim)
    qkv_grad_sum = lax.dot_general(
        attn_in, qkv_grad_flat, CONTRACT_ROWS, preferred_element_type=jnp.float32
    )
    summed = jnp.sum(qkv_grad.astype(jnp.float32), axis=0)
    qv_grad = jnp.stack([summed[:, 0], summed[:, 2]], axis=1).reshape(2 * local_heads * head_dim)
    attn_in_part = lax.dot_general(
        qkv_grad_flat, qkv_full, CONTRACT_COLS, preferred_element_type=jnp.float32
    ).astype(BF16)
    sums = lax.dynamic_update_slice(sums, up_shift_grad[None], (6, 0))
    sums = lax.dynamic_update_slice(sums, qv_grad[None], (7, 0))
    grads = tuple(
        g.astype(BF16).reshape(dp_count, -1, g.shape[-1])
        for g in (qkv_grad_sum, dense_grad)
    )
    block_input_gradient, sums, qkv_out, dense_out = reduce_all(
        dp_count,
        attn_in_part.reshape(4, own_rows, width),
        block_input,
        residual_middle_gradient,
        vec,
        sums,
        grads,
    )
    vectors = lax.dynamic_slice(sums, (0, shard * piece), (6, piece))
    up_shift_out = lax.dynamic_slice(sums, (6, dp_index * up_piece), (1, up_piece))[0]
    qv_out = lax.dynamic_slice(sums, (7, dp_index * qv_piece), (1, qv_piece))[0]
    return (
        block_out,
        block_input_gradient,
        vectors[0],
        vectors[1],
        qkv_out,
        qv_out,
        dense_out,
        vectors[2],
        vectors[3],
        vectors[4],
        up_out,
        up_shift_out,
        down_out,
        vectors[5],
    )


def solution(mesh):
    return jax.shard_map(
        functools.partial(per_device, mesh.shape["dp"]),
        mesh=mesh,
        in_specs=(
            P(("dp", "tensor"), None),
            P("dp"),
            P("dp"),
            P(("dp", "tensor")),
            P(("dp", "tensor")),
            P("dp", "tensor"),
            P(("tensor", "dp")),
            P(("tensor", "dp"), None),
            P(("dp", "tensor")),
            P(("dp", "tensor")),
            P(("dp", "tensor")),
            P("dp", "tensor"),
            P(("tensor", "dp")),
            P(("tensor", "dp"), None),
            P(("dp", "tensor")),
            P(("dp", "tensor"), None),
        ),
        out_specs=(
            P(("dp", "tensor"), None),
            P(("dp", "tensor"), None),
            P(("dp", "tensor")),
            P(("dp", "tensor")),
            P("dp", "tensor"),
            P(("tensor", "dp")),
            P(("tensor", "dp"), None),
            P(("dp", "tensor")),
            P(("dp", "tensor")),
            P(("dp", "tensor")),
            P("dp", "tensor"),
            P(("tensor", "dp")),
            P(("tensor", "dp"), None),
            P(("dp", "tensor")),
        ),
        check_vma=False,
    )
```
